32 devices in a mesh: req: 8 (over z, x), head: 4 (over y, core).
Axes of the slice: x: 2, y: 2, z: 4, core: 2. Of those that a mesh axis runs over, the one named last changes fastest.
Arguments:
- hidden_in: bfloat16 [64, 2048], P('req'), may hold values from -4 to 4
- queries: bfloat16 [64, 2048], P('req', 'head'), may hold values from -7.5 to 7.5
- new_keys: bfloat16 [64, 2048], P('req', 'head'), may hold values from -10 to 10
- new_values: bfloat16 [64, 2048], P('req', 'head'), may hold values from -8 to 8
- key_cache: bfloat16 [64, 1024, 2048], P('req', None, 'head'), may hold values from -4 to 4
- value_cache: bfloat16 [64, 1024, 2048], P('req', None, 'head'), may hold values from -6 to 6
- lengths: int32 [64], P('req'), may hold values from 2 to 1024, as said below
- out_proj: bfloat16 [2048, 2048], P('head'), may hold values from -0.5 to 0.5
- norm_gain: float32 [2048], replicated, may hold values from 0.1 to 1.9
- shared_gate: bfloat16 [5632, 2048], P(('req', 'head')), may hold values from -0.125 to 0.125
- shared_up: bfloat16 [5632, 2048], P(('req', 'head')), may hold values from -0.125 to 0.125
- shared_down: bfloat16 [5632, 2048], P(('req', 'head')), may hold values from -0.078125 to 0.078125
- shared_score: float32 [2048], replicated, may hold values from -0.125 to 0.125
- expert_gate: bfloat16 [8, 2048, 1408], P('req', None, 'head'), may hold values from -0.125 to 0.125
- expert_up: bfloat16 [8, 2048, 1408], P('req', None, 'head'), may hold values from -0.125 to 0.125
- expert_down: bfloat16 [8, 1408, 2048], P('req', 'head'), may hold values from -0.15625 to 0.15625
- expert_ids: int32 [64, 4], P('req'), may hold values from 0 to 7, all different within a row; in each aligned block of 8 rows (0 to 7, 8 to 15, ...) at most 8 rows name the same one
- route_weight: bfloat16 [64, 4], P('req'), may hold values from 0.099609375 to 0.59765625
Outputs:
- layer_out: bfloat16 [64, 2048], P('req')
The draws below stay inside these ranges and needn't reach their ends.
Inputs may be any that keep to these rules, and one draw needn't show every extreme that they name: The first lengths[t] cache positions of request t are live; some request has exactly 1024. `expert_ids`: each row names 4 different experts. Among the 8 rows of one device (aligned blocks) no expert is named by more than 8 rows, and in some blocks one is named by exactly 8.
All inputs are finite; a program needn't handle non-finite values.
Results may differ from the reference program's by a relative error of at most 0.017.
Values may be sent and summed in bfloat16 or wider, within the bound.
A program may use at most 128 MiB of HBM per device.

```python
import math
import jax
import jax.numpy as jnp
import numpy as np
from jax import lax

D = 2048
HEADS = 16
HD = 128
EFF = 1408
SH = 5632
TOPK = 4
B_DEV = 8
MAXLEN = 1024
EXPERTS = 8
TOKENS = 64
CAP = 8


def draw_queries(key, part):
    first_key = jax.random.fold_in(key, 1)
    shape_full = (TOKENS, HEADS * HD)
    return jnp.clip(jax.random.normal(first_key, shape_full, jnp.float32), -4.0, 4.0).astype(jnp.bfloat16)


def draw_key_cache(key, part):
    second_key = jax.random.fold_in(key, 2)
    shape_full = (TOKENS, MAXLEN, HEADS * HD)
    return jnp.clip(jax.random.normal(second_key, shape_full, jnp.float32), -4.0, 4.0).astype(jnp.bfloat16)


def draw_lengths(key, part):
    first_key = jax.random.fold_in(key, 21)
    second_key = jax.random.fold_in(key, 22)
    third_key = jax.random.fold_in(key, 23)
    left = jax.random.randint(first_key, (TOKENS,), 1, MAXLEN + 1, dtype=jnp.int32)
    right = jax.random.randint(second_key, (TOKENS,), 1, MAXLEN + 1, dtype=jnp.int32)
    spans = jnp.maximum(left * right // MAXLEN, 2)
    chosen = jax.random.randint(third_key, (), 0, TOKENS, dtype=jnp.int32)
    return jnp.where(jnp.arange(TOKENS, dtype=jnp.int32) == chosen, MAXLEN, spans).astype(jnp.int32)


def levels(stream_key, shape, shards, least, high):
    def one(dim, parts):
        heights = jax.random.uniform(jax.random.fold_in(jax.random.fold_in(stream_key, 6), dim), (parts,), jnp.float32, least / len(shards), high / len(shards))
        return jnp.repeat(jnp.exp(heights), shape[dim] // parts).reshape((-1,) + (1,) * (len(shape) - dim - 1))

    level = one(*shards[0])
    for cut in shards[1:]:
        level = level * one(*cut)
    return level


def deal_out(stream_key, own, number, rows, count, top, most, skew):
    ranking = jax.random.permutation(stream_key, count)
    packed, ordinary = portions_of(count, rows * top, most, skew, True), portions_of(count, rows * top, most, skew, False)
    places = jnp.arange(count)

    def named(sizes, turn):
        used = int((sizes > 0).sum())
        fixed = max(1, used // 4)
        shifted = fixed + (places - fixed + turn * (used - fixed)) % max(1, count - fixed)
        return jnp.zeros((count,), jnp.int32).at[ranking[jnp.where(places < fixed, places, shifted)]].set(jnp.asarray(sizes, jnp.int32))

    sizes = jnp.where(number % 4 == 0, named(packed, number // 4), named(ordinary, number - number // 4 - 1))
    mixed = jax.random.permutation(jax.random.fold_in(own, 3), count)
    giver, sink = mixed[0:count // 2 * 2:2], mixed[1:count // 2 * 2:2]
    slack = jnp.minimum(sizes[giver] - 1, most - sizes[sink]) // 2
    slack = jnp.where((giver == ranking[0]) | (sink == ranking[0]) | (sizes[sink] == 0), 0, jnp.maximum(slack, 0))
    shifted = jax.random.randint(jax.random.fold_in(own, 4), (count // 2,), 0, 1 << 20) % (slack + 1)
    sizes = sizes.at[giver].add(-shifted).at[sink].add(shifted)
    labels = jnp.searchsorted(jnp.cumsum(sizes), jnp.arange(rows * top), side="right").astype(jnp.int32)
    table = labels.reshape(top, rows).T
    table = table[jax.random.permutation(jax.random.fold_in(own, 1), rows)]
    turn = jax.random.randint(jax.random.fold_in(own, 2), (rows, 1), 0, top)
    return jnp.take_along_axis(table, (jnp.arange(top)[None, :] + turn) % top, axis=1)


def portions_of(count, total, most, skew, full):
    loads = [(1 << 20) // math.isqrt(rank ** skew) + 1 for rank in range(1, count + 1)]
    largest = most if full else min(most, max(-(-total // count), total * loads[0] // sum(loads)))
    least = 1 if total - largest >= count - 1 else 0
    counts, rest = [largest] + [least] * (count - 1), total - largest - least * (count - 1)
    while rest > 0:
        free = [i for i in range(1, count) if counts[i] < largest] or [i for i in range(1, count) if counts[i] < most]
        pool, budget = sum([loads[i] for i in free]), rest
        for i in free:
            addition = min(most - counts[i], max(1, budget * loads[i] // pool), rest)
            counts[i] = counts[i] + addition
            rest = rest - addition
    return np.array(counts)


def gaussian(key, extent, width, most, cuts=(), kind=jnp.bfloat16):
    values = jax.random.normal(key, extent, jnp.float32) * width
    if len(cuts) > 0:
        values = levels(key, extent, cuts, -0.22, 0.18) * values
    return jnp.clip(values, min=-most, max=most).astype(kind)


def setup_inputs(seed: int = 0) -> dict:
    splits = jax.random.split(jax.random.key(seed), 19)
    hidden_in = gaussian(splits[0], (TOKENS, D), 0.5, 4.0, ((0, 8),))
    queries = draw_queries(jax.random.fold_in(splits[18], 71), 0)
    new_keys = gaussian(splits[2], (TOKENS, HEADS * HD), 2.5, 10.0, ((0, 8), (1, 4)))
    new_values = gaussian(splits[3], (TOKENS, HEADS * HD), 1.5, 8.0, ((0, 8), (1, 4)))
    key_cache = draw_key_cache(jax.random.fold_in(splits[18], 71), 0)
    value_cache = gaussian(splits[5], (TOKENS, MAXLEN, HEADS * HD), 1.0, 6.0, ((0, 8), (2, 4)))
    lengths = draw_lengths(jax.random.fold_in(splits[18], 71), 0)
    out_proj = gaussian(splits[7], (HEADS * HD, D), HD ** -0.5, 0.5, ((0, 4),))
    norm_gain = jnp.clip(1.0 + 0.18 * jax.random.normal(splits[8], (D,), jnp.float32), 0.1, 1.9)
    shared_gate = gaussian(splits[9], (SH, D), D ** -0.5, 0.125, ((0, 32),))
    shared_up = gaussian(splits[10], (SH, D), D ** -0.5, 0.125, ((0, 32),))
    shared_down = gaussian(splits[11], (SH, D), SH ** -0.5, 0.078125, ((0, 32),))
    shared_score = gaussian(splits[12], (D,), D ** -0.5, 0.125, (), jnp.float32)
    expert_gate = gaussian(splits[13], (EXPERTS, D, EFF), D ** -0.5, 0.125, ((0, 8), (2, 4)))
    expert_up = gaussian(splits[14], (EXPERTS, D, EFF), D ** -0.5, 0.125, ((0, 8), (2, 4)))
    expert_down = gaussian(splits[15], (EXPERTS, EFF, D), EFF ** -0.5, 0.15625, ((0, 8), (1, 4)))
    expert_ids_keys = jax.random.split(jax.random.fold_in(splits[16], 1), TOKENS // B_DEV)
    expert_ids_turns = jax.random.permutation(jax.random.fold_in(splits[16], 3), TOKENS // B_DEV)
    expert_ids = jax.vmap(lambda own, number: deal_out(jax.random.fold_in(splits[16], 2), own, number, B_DEV, EXPERTS, TOPK, CAP, 2))(expert_ids_keys, expert_ids_turns).reshape((TOKENS, TOPK))
    route_weight = jnp.clip(jnp.exp(math.log(0.59765625) - 1.7917595 * jax.random.uniform(splits[17], (TOKENS, TOPK), jnp.float32) ** levels(splits[17], (TOKENS, TOPK), ((0, 8),), -0.2, 0.2)), 0.099609375, 0.59765625).astype(jnp.bfloat16)
    return dict(hidden_in=hidden_in, queries=queries, new_keys=new_keys, new_values=new_values, key_cache=key_cache, value_cache=value_cache, lengths=lengths, out_proj=out_proj, norm_gain=norm_gain, shared_gate=shared_gate, shared_up=shared_up, shared_down=shared_down, shared_score=shared_score, expert_gate=expert_gate, expert_up=expert_up, expert_down=expert_down, expert_ids=expert_ids, route_weight=route_weight)


EPSILON = 1e-06

def attend(queries, new_keys, new_values, key_cache, value_cache, lengths):
    row_count = queries.shape[0]
    key_span = key_cache.shape[1]
    score_scale = HD ** (-0.5)
    query_heads = queries.reshape(row_count, HEADS, HD).astype(jnp.float32)
    own_keys = new_keys.reshape(row_count, HEADS, HD).astype(jnp.float32)
    own_values = new_values.reshape(row_count, HEADS, HD).astype(jnp.float32)
    cache_keys = key_cache.reshape(row_count, key_span, HEADS, HD).astype(jnp.float32)
    cache_values = value_cache.reshape(row_count, key_span, HEADS, HD).astype(jnp.float32)
    scores = jnp.einsum('bhd,blhd->bhl', query_heads, cache_keys) * score_scale
    own_score = jnp.einsum('bhd,bhd->bh', query_heads, own_keys) * score_scale
    live_keys = jnp.arange(key_span, dtype=jnp.int32)[None, None, :] < lengths[:, None, None]
    highest = jnp.maximum(lax.optimization_barrier(jnp.max(jnp.where(live_keys, scores, -1e+30), axis=-1)), own_score)
    weights = jnp.where(live_keys, jnp.exp(scores - highest[..., None]), 0.0)
    own_weight = jnp.exp(own_score - highest)
    totals = lax.optimization_barrier(jnp.sum(weights, axis=-1)) + own_weight
    probs = (weights / totals[..., None]).astype(jnp.bfloat16)
    own_prob = (own_weight / totals).astype(jnp.bfloat16)
    mixed = jnp.einsum('bhl,blhd->bhd', probs.astype(jnp.float32), cache_values)
    mixed = mixed + own_prob.astype(jnp.float32)[..., None] * own_values
    return mixed.astype(jnp.bfloat16).reshape(row_count, HEADS * HD)

def normalize(residual, norm_gain):
    values = residual.astype(jnp.float32)
    mean_square = lax.optimization_barrier(jnp.mean(values * values, axis=-1, keepdims=True))
    return (values * lax.rsqrt(mean_square + EPSILON) * norm_gain).astype(jnp.bfloat16)

def reference(hidden_in, queries, new_keys, new_values, key_cache, value_cache, lengths, out_proj, norm_gain, shared_gate, shared_up, shared_down, shared_score, expert_gate, expert_up, expert_down, expert_ids, route_weight):
    block_count = TOKENS // B_DEV
    pieces = (queries, new_keys, new_values, key_cache, value_cache, lengths)
    stacked = tuple((array.reshape((block_count, B_DEV) + array.shape[1:]) for array in pieces))

    def block_attend(block):
        return attend(*block)
    attended = lax.map(block_attend, stacked).reshape(TOKENS, HEADS * HD)
    attn_out = jnp.dot(attended, out_proj, preferred_element_type=jnp.float32)
    residual = (hidden_in.astype(jnp.float32) + attn_out).astype(jnp.bfloat16)
    normed = normalize(residual, norm_gain)
    normed_wide = normed.astype(jnp.float32)
    contract = (((1,), (1,)), ((), ()))
    shared_g = lax.dot_general(normed, shared_gate, contract, preferred_element_type=jnp.float32)
    shared_u = lax.dot_general(normed, shared_up, contract, preferred_element_type=jnp.float32)
    shared_hidden = (jax.nn.silu(shared_g) * shared_u).astype(jnp.bfloat16)
    shared_sum = jnp.dot(shared_hidden, shared_down, preferred_element_type=jnp.float32)
    gate_scale = jax.nn.sigmoid(jnp.dot(normed_wide, shared_score, precision=lax.Precision.HIGHEST))

    def one_expert(total, block):
        gate_w, up_w, down_w, index = block
        gate = jnp.dot(normed_wide, gate_w.astype(jnp.float32), precision=lax.Precision.HIGHEST)
        up_proj = jnp.dot(normed_wide, up_w.astype(jnp.float32), precision=lax.Precision.HIGHEST)
        inner = (jax.nn.silu(gate) * up_proj).astype(jnp.bfloat16)
        result = jnp.dot(inner.astype(jnp.float32), down_w.astype(jnp.float32), precision=lax.Precision.HIGHEST)
        weight = lax.optimization_barrier(jnp.sum(jnp.where(expert_ids == index, route_weight.astype(jnp.float32), 0.0), axis=1))
        return (total + weight[:, None] * result, None)
    start_total = jnp.zeros((TOKENS, D), jnp.float32)
    routed, _ = lax.scan(one_expert, start_total, (expert_gate, expert_up, expert_down, jnp.arange(EXPERTS, dtype=jnp.int32)))
    layer_out = residual.astype(jnp.float32) + gate_scale[:, None] * shared_sum + routed
    return layer_out.astype(jnp.bfloat16)
```

```python
import functools

import jax
import jax.numpy as jnp
from jax import lax
from jax.experimental import pallas as pl
from jax.experimental.pallas import tpu as pltpu
from jax.sharding import PartitionSpec as P

PARTS = 2
AHEAD = 6
HD = 128
EPSILON = 1e-06
MESH = pl.DeviceIdType.MESH
BF16, F32 = jnp.bfloat16, jnp.float32
ROWS_BY_ROWS = (((1,), (1,)), ((), ()))


def silu(x):
    return x / (1.0 + jnp.exp(-x))


def layer_kernel(
    req_count, head_count,
    lengths_hbm, q_hbm, nk_hbm, nv_hbm, k_hbm, v_hbm, proj_hbm,
    hid_hbm, gain_hbm, score_hbm, ids_hbm, rw_hbm,
    sg_hbm, su_hbm, sd_hbm, eg_hbm, eu_hbm, ed_hbm,
    out_ref,
    lengths_ref, new_ref, hid_ref, gains, ids_ref, rw_ref,
    k_buf, v_buf, proj_buf, expert, shared_w, load_sems, k_sem, v_sem,
    attended, w_own, w_in, w_part, x_own, x_other, d_own,
    pair1_out, pair1_in, mine1, land1, fwd_out, fwd_in,
    pair2_out, pair2_in, send2, land2, fin_out, fin_in,
    w_sems, part_sems,
):
    rows, model = hid_ref.shape
    parts = mine1.shape[0]
    toks = rows // parts
    half = model // 2
    lines = head_count // 2
    me_r = lax.axis_index("req")
    me_h = lax.axis_index("head")
    me_y = lax.div(me_h, 2)
    me_c = lax.rem(me_h, 2)
    pair = me_y * 2 + 1 - me_c
    own = pl.ds(pl.multiple_of(me_c * half, 128), half)
    other = pl.ds(pl.multiple_of((1 - me_c) * half, 128), half)
    bits = []
    while (1 << len(bits)) < req_count:
        bits.append(lax.rem(lax.div(me_r, 1 << len(bits)), 2))

    def row(j):
        return sum(
            ((1 - bit) if (j >> i) & 1 else bit) * (1 << i) for i, bit in enumerate(bits)
        )

    peer_rows = [row(j) for j in range(req_count)]
    lines_at = [lax.rem(me_y + y, lines) * 2 + me_c for y in range(lines)]
    back_at = [lax.rem(me_y + lines - y, lines) * 2 + me_c for y in range(lines)]
    steps = [
        (j, y) for j in reversed(range(req_count)) for y in reversed(range(lines)) if j + y > 0
    ]

    def remote(src, dst, send, recv, r, h):
        return pltpu.make_async_remote_copy(
            src_ref=src, dst_ref=dst, send_sem=send, recv_sem=recv,
            device_id=(r, h), device_id_type=MESH,
        )

    barrier = pltpu.get_barrier_semaphore()
    for j, y in steps:
        pl.semaphore_signal(
            barrier, inc=1, device_id=(peer_rows[j], back_at[y]), device_id_type=MESH
        )
    pl.semaphore_signal(barrier, inc=1, device_id=(me_r, pair), device_id_type=MESH)

    def copies(sem, *pairs):
        return [pltpu.make_async_copy(src, dst, load_sems.at[sem]) for src, dst in pairs]

    new_loads = copies(0, (q_hbm, new_ref.at[0]), (nk_hbm, new_ref.at[1]), (nv_hbm, new_ref.at[2]))
    small = (
        copies(1, (lengths_hbm, lengths_ref)) + copies(2, (ids_hbm, ids_ref))
        + copies(3, (rw_hbm, rw_ref)) + copies(4, (hid_hbm, hid_ref))
    )
    gain_loads = copies(5, (gain_hbm, gains.at[0]), (score_hbm, gains.at[1]))
    proj_load = copies(6, (proj_hbm, proj_buf))
    expert_loads = copies(
        7, (eg_hbm.at[0], expert.at[0]), (eu_hbm.at[0], expert.at[1]), (ed_hbm.at[0], expert.at[2])
    )
    shared_loads = copies(
        8, (sg_hbm, shared_w.at[0]), (su_hbm, shared_w.at[1]), (sd_hbm, shared_w.at[2])
    )
    PAIR = 2

    def cache_load(hbm, buf, sem, b):
        rows_at = pl.ds(b, PAIR)
        return pltpu.make_async_copy(hbm.at[rows_at], buf.at[rows_at], sem.at[b // PAIR])

    k_load = [cache_load(k_hbm, k_buf, k_sem, b) for b in range(0, rows, PAIR)]
    v_load = [cache_load(v_hbm, v_buf, v_sem, b) for b in range(0, rows, PAIR)]
    queue = [k_load[0]]
    for i in range(len(v_load)):
        queue += k_load[i + 1:i + 2]
        if i == toks // PAIR - 1:
            queue += proj_load
        queue.append(v_load[i])
    queue += expert_loads + shared_loads
    issued = [0]

    def issue(upto):
        while issued[0] < min(upto, len(queue)):
            queue[issued[0]].start()
            issued[0] += 1

    def landed(copy):
        copy.wait()
        issue(next(i for i, c in enumerate(queue) if c is copy) + 1 + AHEAD)

    for load in new_loads + small + gain_loads:
        load.start()
    issue(AHEAD)
    pltpu.make_async_copy(new_ref, new_ref, load_sems.at[0]).wait()
    for load in small:
        load.wait()
    pltpu.make_async_copy(gains, gains, load_sems.at[5]).wait()

    span, width = k_buf.shape[1:]
    scale = HD ** (-0.5)
    group = max(8, width // HD)
    own_head = (
        lax.broadcasted_iota(jnp.int32, (group, width), 0)
        == lax.broadcasted_iota(jnp.int32, (group, width), 1) // HD
    )
    position = lax.broadcasted_iota(jnp.int32, (group, span), 1)
    queries = new_ref[0].astype(F32)
    own_keys = new_ref[1].astype(F32)
    own_values = new_ref[2].astype(F32)

    def score(b):
        spread = jnp.where(own_head, queries[b:b + 1, :], 0.0)
        scores = lax.dot_general(
            spread.astype(BF16), k_buf[b], ROWS_BY_ROWS, preferred_element_type=F32
        )
        own_score = jnp.sum(spread * own_keys[b:b + 1, :], axis=1, keepdims=True)
        return scores, own_score

    def mix(b, scored):
        scores, own_score = scored
        alive = position < lengths_ref[b]
        scores = jnp.where(alive, scores, -1e30)
        highest = jnp.maximum(jnp.max(scores, axis=1, keepdims=True), own_score)
        exps = jnp.exp((scores - highest) * scale)
        own_exp = jnp.exp((own_score - highest) * scale)
        mixed = jnp.dot(exps.astype(BF16), v_buf[b], preferred_element_type=F32)
        norm = jnp.sum(exps, axis=1, keepdims=True) + own_exp
        mixed = (mixed + own_exp * own_values[b:b + 1, :]) / norm
        attended[b:b + 1, :] = jnp.sum(jnp.where(own_head, mixed, 0.0), axis=0, keepdims=True)

    scored = {}

    def attend(b):
        if b < rows:
            landed(k_load[b // PAIR])
        if b >= PAIR:
            landed(v_load[b // PAIR - 1])
        for i in range(b, b + PAIR):
            if i < rows:
                scored[i] = score(i)
            if i >= PAIR:
                mix(i - PAIR, scored.pop(i - PAIR))

    def route_table():
        lane = lax.broadcasted_iota(jnp.int32, (rows, 128), 1).astype(F32)
        table = jnp.zeros((rows, 128), F32)
        route = rw_ref[...].astype(F32)
        ids = ids_ref[...].astype(F32)
        diagonal = (
            lax.broadcasted_iota(jnp.int32, (rows, rows), 0)
            == lax.broadcasted_iota(jnp.int32, (rows, rows), 1)
        )
        for k in range(ids.shape[0]):
            chosen = jnp.sum(jnp.where(diagonal, ids[k:k + 1, :], 0.0), axis=1, keepdims=True)
            share = jnp.sum(jnp.where(diagonal, route[k:k + 1, :], 0.0), axis=1, keepdims=True)
            table = table + jnp.where(chosen == lane, share, 0.0)
        w_own[...] = table

    def route_copies():
        for j in reversed(range(1, req_count)):
            remote(w_own, w_in.at[j - 1], w_sems.at[0], w_sems.at[1], peer_rows[j], me_h).start()

    def all_sent(ref, sem):
        remote(ref, ref, sem, sem, me_r, pair).wait_send()

    def all_here(ref, sem):
        remote(ref, ref, sem, sem, me_r, pair).wait_recv()

    def rows_of(p):
        return slice(p * toks, (p + 1) * toks)

    def pair_copy(p, src, dst, sem):
        return remote(
            src.at[p], dst.at[p], part_sems.at[p, sem], part_sems.at[p, sem + 1], me_r, pair
        )

    kept = {}

    def project(p):
        mixed = attended[rows_of(p), :].astype(BF16)
        pair1_out[p] = jnp.dot(mixed, proj_buf[:, other], preferred_element_type=F32)
        pair_copy(p, pair1_out, pair1_in, 0).start()
        hidden = jnp.where(me_y == 0, hid_ref[:, own].astype(F32), 0.0)
        kept[p] = (
            jnp.dot(mixed, proj_buf[:, own], preferred_element_type=F32) + hidden[rows_of(p)]
        )

    def spread_out(p):
        pair_copy(p, pair1_out, pair1_in, 0).wait_recv()
        mine1[p] = (kept.pop(p) + pair1_in[p]).astype(BF16)
        for j, y in steps:
            remote(
                mine1.at[p], land1.at[p, j * lines + y - 1], part_sems.at[p, 2],
                part_sems.at[p, 3], peer_rows[j], lines_at[y],
            ).start()

    def collect(p):
        all_here(land1.at[p], part_sems.at[p, 3])
        for j in range(req_count):
            total = None
            for y in range(lines):
                block = land1[p, j * lines + y - 1] if j + y > 0 else mine1[p]
                block = block.astype(F32)
                total = block if total is None else total + block
            resid = total.astype(BF16)
            fwd_out[p, j] = resid
            x_own[p, j * toks:(j + 1) * toks, :] = resid.astype(F32)
        pair_copy(p, fwd_out, fwd_in, 4).start()

    def half_terms(x, cols):
        square = jnp.sum(x * x, axis=1, keepdims=True)
        gained = (x * gains[0, :, cols]).astype(BF16)
        logit = jnp.sum(gained.astype(F32) * gains[1, :, cols], axis=1, keepdims=True)
        return [square, logit] + [
            lax.dot_general(gained, w[i, :, cols], ROWS_BY_ROWS, preferred_element_type=F32)
            for w in (expert, shared_w) for i in range(2)
        ]

    def experts(p):
        first = half_terms(x_own[p], own)
        pair_copy(p, fwd_out, fwd_in, 4).wait_recv()
        for j in range(req_count):
            x_other[p, j * toks:(j + 1) * toks, :] = fwd_in[p, j].astype(F32)
        second = half_terms(x_other[p], other)
        square, logit, g, u, shared_g, shared_u = [a + b for a, b in zip(first, second)]
        inverse = lax.rsqrt(square / model + EPSILON)
        gate_scale = 1.0 / (1.0 + jnp.exp(-logit * inverse))
        lane = lax.broadcasted_iota(jnp.int32, w_part.shape[1:], 1)
        weight = jnp.sum(jnp.where(lane == me_r, w_part[p], 0.0), axis=1, keepdims=True)
        inner = (silu(g * inverse) * (u * (inverse * weight))).astype(BF16)
        hidden = (silu(shared_g * inverse) * (shared_u * (inverse * gate_scale))).astype(BF16)

        def down(cols):
            return (
                jnp.dot(inner, expert[2, :, cols], preferred_element_type=F32)
                + jnp.dot(hidden, shared_w[2, :, cols], preferred_element_type=F32)
            )

        pair2_out[p] = down(other).astype(BF16)
        pair_copy(p, pair2_out, pair2_in, 6).start()
        d_own[p] = down(own)

    def give_back(p):
        pair_copy(p, pair2_out, pair2_in, 6).wait_recv()
        d_own[p] = d_own[p] + pair2_in[p].astype(F32)
        for j in reversed(range(req_count)):
            send2[p, j] = d_own[p, j * toks:(j + 1) * toks, :].astype(BF16)
            for y in reversed(range(lines)):
                if j + y > 0:
                    remote(
                        send2.at[p, j], land2.at[p, j * lines + y - 1], part_sems.at[p, 8],
                        part_sems.at[p, 9], peer_rows[j], lines_at[y],
                    ).start()

    def combine(p):
        total = fwd_out[p, 0].astype(F32) + d_own[p, 0:toks, :]
        all_here(land2.at[p], part_sems.at[p, 9])
        for i in range(land2.shape[1]):
            total = total + land2[p, i].astype(F32)
        fin_out[p] = total.astype(BF16)
        pair_copy(p, fin_out, fin_in, 10).start()

    def finish():
        for p in range(parts):
            pair_copy(p, fin_out, fin_in, 10).wait_recv()
        for cols, ref in ((own, fin_out), (other, fin_in)):
            blocks = [ref[p].astype(F32) for p in range(parts)]
            whole = blocks[0] if parts == 1 else jnp.concatenate(blocks, axis=0)
            out_ref[:, cols] = whole.astype(BF16)

    route_table()
    for b in range(0, toks + PAIR, PAIR):
        attend(b)
    landed(proj_load[0])
    pl.semaphore_wait(barrier, len(steps) + 1)
    project(0)
    route_copies()
    if parts > 1:
        attend(toks + PAIR)
    spread_out(0)
    if parts > 1:
        for b in range(toks + 2 * PAIR, rows + PAIR, PAIR):
            attend(b)
        project(1)
        spread_out(1)
    issue(len(queue))
    all_here(w_in, w_sems.at[1])
    for p in range(parts):
        for j in range(req_count):
            table = w_own if j == 0 else w_in.at[j - 1]
            w_part[p, j * toks:(j + 1) * toks, :] = table[rows_of(p), :]
    for p in range(parts):
        collect(p)
        if p == 0:
            pltpu.make_async_copy(expert, expert, load_sems.at[7]).wait()
            pltpu.make_async_copy(shared_w, shared_w, load_sems.at[8]).wait()
        experts(p)
        give_back(p)
    for p in range(parts):
        combine(p)
    finish()
    all_sent(w_in, w_sems.at[0])
    for p in range(parts):
        all_sent(land1.at[p], part_sems.at[p, 2])
        all_sent(land2.at[p], part_sems.at[p, 8])
        for src, dst, sem in (
            (pair1_out, pair1_in, 0), (fwd_out, fwd_in, 4), (pair2_out, pair2_in, 6),
            (fin_out, fin_in, 10),
        ):
            pair_copy(p, src, dst, sem).wait_send()


VMEM_SPEC = pl.BlockSpec(memory_space=pltpu.VMEM)
HBM_SPEC = pl.BlockSpec(memory_space=pltpu.HBM)


def per_device(
    req_count, head_count,
    hidden_in, queries, new_keys, new_values, key_cache, value_cache, lengths, out_proj,
    norm_gain, shared_gate, shared_up, shared_down, shared_score, expert_gate, expert_up,
    expert_down, expert_ids, route_weight,
):
    rows, model = hidden_in.shape
    span, width = key_cache.shape[1:]
    dma, vmem = pltpu.SemaphoreType.DMA, pltpu.VMEM
    parts, lines, half = PARTS, head_count // 2, model // 2
    toks = rows // parts
    tokens = req_count * toks
    return pl.pallas_call(
        functools.partial(layer_kernel, req_count, head_count),
        out_shape=jax.ShapeDtypeStruct((rows, model), BF16),
        in_specs=[HBM_SPEC] * 18,
        out_specs=VMEM_SPEC,
        scratch_shapes=[
            pltpu.SMEM((rows,), jnp.int32),
            vmem((3, rows, width), BF16),
            vmem((rows, model), BF16),
            vmem((2, 1, model), F32),
            vmem(expert_ids.shape[::-1], jnp.int32),
            vmem(route_weight.shape[::-1], BF16),
            vmem((rows, span, width), BF16),
            vmem((rows, span, width), BF16),
            vmem(out_proj.shape, BF16),
            vmem((3,) + expert_down.shape[1:], BF16),
            vmem((3,) + shared_down.shape, BF16),
            dma((9,)), dma((rows // 2,)), dma((rows // 2,)),
            vmem((rows, width), F32),
            vmem((rows, 128), F32),
            vmem((req_count - 1, rows, 128), F32),
            vmem((parts, tokens, 128), F32),
            vmem((parts, tokens, half), F32),
            vmem((parts, tokens, half), F32),
            vmem((parts, tokens, half), F32),
            vmem((parts, toks, half), F32),
            vmem((parts, toks, half), F32),
            vmem((parts, toks, half), BF16),
            vmem((parts, req_count * lines - 1, toks, half), BF16),
            vmem((parts, req_count, toks, half), BF16),
            vmem((parts, req_count, toks, half), BF16),
            vmem((parts, tokens, half), BF16),
            vmem((parts, tokens, half), BF16),
            vmem((parts, req_count, toks, half), BF16),
            vmem((parts, req_count * lines - 1, toks, half), BF16),
            vmem((parts, toks, half), BF16),
            vmem((parts, toks, half), BF16),
            dma((2,)), dma((parts, 12)),
        ],
        compiler_params=pltpu.CompilerParams(
            vmem_limit_bytes=64 << 20, collective_id=0, has_side_effects=True
        ),
        name="layer",
    )(
        lengths, queries, new_keys, new_values, key_cache, value_cache, out_proj,
        hidden_in, norm_gain.reshape(1, model), shared_score.reshape(1, model),
        expert_ids.T, route_weight.T,
        shared_gate, shared_up, shared_down,
        jnp.swapaxes(expert_gate, 1, 2), jnp.swapaxes(expert_up, 1, 2), expert_down,
    )


def solution(mesh):
    in_specs = (
        P("req", None),
        P("req", "head"),
        P("req", "head"),
        P("req", "head"),
        P("req", None, "head"),
        P("req", None, "head"),
        P("req"),
        P("head", None),
        P(),
        P(("req", "head"), None),
        P(("req", "head"), None),
        P(("req", "head"), None),
        P(),
        P("req", None, "head"),
        P("req", None, "head"),
        P("req", "head", None),
        P("req", None),
        P("req", None),
    )
    body = functools.partial(per_device, mesh.shape["req"], mesh.shape["head"])
    return jax.shard_map(
        body, mesh=mesh, in_specs=in_specs, out_specs=P("req", None), check_vma=False
    )
```

```python
import functools

import jax
import jax.numpy as jnp
from jax import lax
from jax.experimental import pallas as pl
from jax.experimental.pallas import tpu as pltpu
from jax.sharding import PartitionSpec as P

PARTS = 2
AHEAD = 6
VM = 63
ORD = 1
SM = 1
EARLY = 1
HD = 128
EPSILON = 1e-06
MESH = pl.DeviceIdType.MESH
BF16, F32 = jnp.bfloat16, jnp.float32
ROWS_BY_ROWS = (((1,), (1,)), ((), ()))


def silu(x):
    return x / (1.0 + jnp.exp(-x))


def layer_kernel(
    req_count, head_count,
    lengths_hbm, q_hbm, nk_hbm, nv_hbm, k_hbm, v_hbm, proj_hbm,
    hid_hbm, gain_hbm, score_hbm, ids_hbm, rw_hbm,
    sg_hbm, su_hbm, sd_hbm, eg_hbm, eu_hbm, ed_hbm,
    out_ref,
    lengths_ref, new_ref, hid_ref, gains, ids_ref, rw_ref,
    k_buf, v_buf, proj_buf, expert, shared_w, load_sems, k_sem, v_sem,
    attended, w_own, w_in, w_part, x_own, x_other, d_own,
    pair1_out, pair1_in, mine1, land1, fwd_out, fwd_in,
    pair2_out, pair2_in, send2, land2, fin_out, fin_in,
    w_sems, part_sems,
):
    rows, model = hid_ref.shape
    parts = mine1.shape[0]
    toks = rows // parts
    half = model // 2
    lines = head_count // 2
    me_r = lax.axis_index("req")
    me_h = lax.axis_index("head")
    me_y = lax.div(me_h, 2)
    me_c = lax.rem(me_h, 2)
    pair = me_y * 2 + 1 - me_c
    own = pl.ds(pl.multiple_of(me_c * half, 128), half)
    other = pl.ds(pl.multiple_of((1 - me_c) * half, 128), half)
    bits = []
    while (1 << len(bits)) < req_count:
        bits.append(lax.rem(lax.div(me_r, 1 << len(bits)), 2))

    def row(j):
        return sum(
            ((1 - bit) if (j >> i) & 1 else bit) * (1 << i) for i, bit in enumerate(bits)
        )

    peer_rows = [row(j) for j in range(req_count)]
    lines_at = [lax.rem(me_y + y, lines) * 2 + me_c for y in range(lines)]
    back_at = [lax.rem(me_y + lines - y, lines) * 2 + me_c for y in range(lines)]
    steps = [
        (j, y) for j in reversed(range(req_count)) for y in reversed(range(lines)) if j + y > 0
    ]

    def remote(src, dst, send, recv, r, h):
        return pltpu.make_async_remote_copy(
            src_ref=src, dst_ref=dst, send_sem=send, recv_sem=recv,
            device_id=(r, h), device_id_type=MESH,
        )

    def copies(sem, *pairs):
        return [pltpu.make_async_copy(src, dst, load_sems.at[sem]) for src, dst in pairs]

    new_loads = copies(0, (q_hbm, new_ref.at[0]), (nk_hbm, new_ref.at[1]), (nv_hbm, new_ref.at[2]))
    small = (
        copies(1, (lengths_hbm, lengths_ref)) + copies(2, (ids_hbm, ids_ref))
        + copies(3, (rw_hbm, rw_ref)) + copies(4, (hid_hbm, hid_ref))
    )
    gain_loads = copies(5, (gain_hbm, gains.at[0]), (score_hbm, gains.at[1]))
    proj_load = copies(6, (proj_hbm, proj_buf))
    expert_loads = copies(
        7, (eg_hbm.at[0], expert.at[0]), (eu_hbm.at[0], expert.at[1]), (ed_hbm.at[0], expert.at[2])
    )
    shared_loads = copies(
        8, (sg_hbm, shared_w.at[0]), (su_hbm, shared_w.at[1]), (sd_hbm, shared_w.at[2])
    )
    PAIR = 2

    def cache_load(hbm, buf, sem, b):
        rows_at = pl.ds(b, PAIR)
        return pltpu.make_async_copy(hbm.at[rows_at], buf.at[rows_at], sem.at[b // PAIR])

    k_load = [cache_load(k_hbm, k_buf, k_sem, b) for b in range(0, rows, PAIR)]
    v_load = [cache_load(v_hbm, v_buf, v_sem, b) for b in range(0, rows, PAIR)]
    queue = [k_load[0]]
    for i in range(len(v_load)):
        queue += k_load[i + 1:i + 2]
        if i == toks // PAIR - 1:
            queue += proj_load
        queue.append(v_load[i])
    queue += expert_loads + shared_loads
    issued = [0]

    def issue(upto):
        while issued[0] < min(upto, len(queue)):
            queue[issued[0]].start()
            issued[0] += 1

    def landed(copy):
        copy.wait()
        issue(next(i for i, c in enumerate(queue) if c is copy) + 1 + AHEAD)

    if EARLY: issue(2)
    for load in new_loads + small + gain_loads:
        load.start()
    issue(AHEAD)
    barrier = pltpu.get_barrier_semaphore()
    for j, y in steps:
        pl.semaphore_signal(
            barrier, inc=1, device_id=(peer_rows[j], back_at[y]), device_id_type=MESH
        )
    pl.semaphore_signal(barrier, inc=1, device_id=(me_r, pair), device_id_type=MESH)

    pltpu.make_async_copy(new_ref, new_ref, load_sems.at[0]).wait()
    for load in small:
        load.wait()
    pltpu.make_async_copy(gains, gains, load_sems.at[5]).wait()

    span, width = k_buf.shape[1:]
    scale = HD ** (-0.5)
    group = max(8, width // HD)
    own_head = (
        lax.broadcasted_iota(jnp.int32, (group, width), 0)
        == lax.broadcasted_iota(jnp.int32, (group, width), 1) // HD
    )
    position = lax.broadcasted_iota(jnp.int32, (group, span), 1)
    queries = new_ref[0].astype(F32)
    own_keys = new_ref[1].astype(F32)
    own_values = new_ref[2].astype(F32)

    if SM == 0:
        def score(b):
            spread = jnp.where(own_head, queries[b:b + 1, :], 0.0)
            scores = lax.dot_general(
                spread.astype(BF16), k_buf[b], ROWS_BY_ROWS, preferred_element_type=F32
            )
            own_score = jnp.sum(spread * own_keys[b:b + 1, :], axis=1, keepdims=True)
            return scores, own_score

        def mix(b, scored):
            scores, own_score = scored
            alive = position < lengths_ref[b]
            scores = jnp.where(alive, scores, -1e30)
            highest = jnp.maximum(jnp.max(scores, axis=1, keepdims=True), own_score)
            exps = jnp.exp((scores - highest) * scale)
            own_exp = jnp.exp((own_score - highest) * scale)
            mixed = jnp.dot(exps.astype(BF16), v_buf[b], preferred_element_type=F32)
            norm = jnp.sum(exps, axis=1, keepdims=True) + own_exp
            mixed = (mixed + own_exp * own_values[b:b + 1, :]) / norm
            attended[b:b + 1, :] = jnp.sum(jnp.where(own_head, mixed, 0.0), axis=0, keepdims=True)
    else:
        def score(b):
            spread = jnp.where(own_head, queries[b:b + 1, :], 0.0)
            scores = lax.dot_general(
                spread.astype(BF16), k_buf[b], ROWS_BY_ROWS, preferred_element_type=F32
            )
            own_score = jnp.sum(spread * own_keys[b:b + 1, :], axis=1, keepdims=True)
            scores = jnp.where(position < lengths_ref[b], scores, -1e30)
            highest = jnp.maximum(jnp.max(scores, axis=1, keepdims=True), own_score)
            exps = jnp.exp((scores - highest) * scale)
            own_exp = jnp.exp((own_score - highest) * scale)
            share = 1.0 / (jnp.sum(exps, axis=1, keepdims=True) + own_exp)
            own_part = jnp.sum(
                jnp.where(own_head, own_exp * own_values[b:b + 1, :], 0.0) * share,
                axis=0, keepdims=True,
            )
            return exps.astype(BF16), share, own_part

        def mix(b, scored):
            exps, share, own_part = scored
            mixed = jnp.dot(exps, v_buf[b], preferred_element_type=F32)
            mixed = jnp.where(own_head, mixed * share, 0.0)
            attended[b:b + 1, :] = jnp.sum(mixed, axis=0, keepdims=True) + own_part

    scored = {}

    def attend(b):
        if b < rows:
            landed(k_load[b // PAIR])
        if b >= PAIR:
            landed(v_load[b // PAIR - 1])
        for i in range(b, b + PAIR):
            if i < rows:
                scored[i] = score(i)
            if i >= PAIR:
                mix(i - PAIR, scored.pop(i - PAIR))

    def route_table():
        lane = lax.broadcasted_iota(jnp.int32, (rows, 128), 1).astype(F32)
        table = jnp.zeros((rows, 128), F32)
        route = rw_ref[...].astype(F32)
        ids = ids_ref[...].astype(F32)
        diagonal = (
            lax.broadcasted_iota(jnp.int32, (rows, rows), 0)
            == lax.broadcasted_iota(jnp.int32, (rows, rows), 1)
        )
        for k in range(ids.shape[0]):
            chosen = jnp.sum(jnp.where(diagonal, ids[k:k + 1, :], 0.0), axis=1, keepdims=True)
            share = jnp.sum(jnp.where(diagonal, route[k:k + 1, :], 0.0), axis=1, keepdims=True)
            table = table + jnp.where(chosen == lane, share, 0.0)
        w_own[...] = table

    def route_copies():
        for j in reversed(range(1, req_count)):
            remote(w_own, w_in.at[j - 1], w_sems.at[0], w_sems.at[1], peer_rows[j], me_h).start()

    def all_sent(ref, sem):
        remote(ref, ref, sem, sem, me_r, pair).wait_send()

    def all_here(ref, sem):
        remote(ref, ref, sem, sem, me_r, pair).wait_recv()

    def rows_of(p):
        return slice(p * toks, (p + 1) * toks)

    def pair_copy(p, src, dst, sem):
        return remote(
            src.at[p], dst.at[p], part_sems.at[p, sem], part_sems.at[p, sem + 1], me_r, pair
        )

    kept = {}

    def project(p):
        mixed = attended[rows_of(p), :].astype(BF16)
        pair1_out[p] = jnp.dot(mixed, proj_buf[:, other], preferred_element_type=F32)
        pair_copy(p, pair1_out, pair1_in, 0).start()
        hidden = jnp.where(me_y == 0, hid_ref[:, own].astype(F32), 0.0)
        kept[p] = (
            jnp.dot(mixed, proj_buf[:, own], preferred_element_type=F32) + hidden[rows_of(p)]
        )

    def spread_out(p):
        pair_copy(p, pair1_out, pair1_in, 0).wait_recv()
        mine1[p] = (kept.pop(p) + pair1_in[p]).astype(BF16)
        for j, y in steps:
            remote(
                mine1.at[p], land1.at[p, j * lines + y - 1], part_sems.at[p, 2],
                part_sems.at[p, 3], peer_rows[j], lines_at[y],
            ).start()

    def collect(p):
        all_here(land1.at[p], part_sems.at[p, 3])
        for j in range(req_count):
            total = None
            for y in range(lines):
                block = land1[p, j * lines + y - 1] if j + y > 0 else mine1[p]
                block = block.astype(F32)
                total = block if total is None else total + block
            resid = total.astype(BF16)
            fwd_out[p, j] = resid
            x_own[p, j * toks:(j + 1) * toks, :] = resid.astype(F32)
        pair_copy(p, fwd_out, fwd_in, 4).start()

    def half_terms(x, cols):
        square = jnp.sum(x * x, axis=1, keepdims=True)
        gained = (x * gains[0, :, cols]).astype(BF16)
        logit = jnp.sum(gained.astype(F32) * gains[1, :, cols], axis=1, keepdims=True)
        return [square, logit] + [
            lax.dot_general(gained, w[i, :, cols], ROWS_BY_ROWS, preferred_element_type=F32)
            for w in (expert, shared_w) for i in range(2)
        ]

    def experts(p):
        first = half_terms(x_own[p], own)
        pair_copy(p, fwd_out, fwd_in, 4).wait_recv()
        for j in range(req_count):
            x_other[p, j * toks:(j + 1) * toks, :] = fwd_in[p, j].astype(F32)
        second = half_terms(x_other[p], other)
        square, logit, g, u, shared_g, shared_u = [a + b for a, b in zip(first, second)]
        inverse = lax.rsqrt(square / model + EPSILON)
        gate_scale = 1.0 / (1.0 + jnp.exp(-logit * inverse))
        lane = lax.broadcasted_iota(jnp.int32, w_part.shape[1:], 1)
        weight = jnp.sum(jnp.where(lane == me_r, w_part[p], 0.0), axis=1, keepdims=True)
        inner = (silu(g * inverse) * (u * (inverse * weight))).astype(BF16)
        hidden = (silu(shared_g * inverse) * (shared_u * (inverse * gate_scale))).astype(BF16)

        def down(cols):
            return (
                jnp.dot(inner, expert[2, :, cols], preferred_element_type=F32)
                + jnp.dot(hidden, shared_w[2, :, cols], preferred_element_type=F32)
            )

        pair2_out[p] = down(other).astype(BF16)
        pair_copy(p, pair2_out, pair2_in, 6).start()
        d_own[p] = down(own)

    def give_back(p):
        pair_copy(p, pair2_out, pair2_in, 6).wait_recv()
        d_own[p] = d_own[p] + pair2_in[p].astype(F32)
        for j in reversed(range(req_count)):
            send2[p, j] = d_own[p, j * toks:(j + 1) * toks, :].astype(BF16)
            for y in reversed(range(lines)):
                if j + y > 0:
                    remote(
                        send2.at[p, j], land2.at[p, j * lines + y - 1], part_sems.at[p, 8],
                        part_sems.at[p, 9], peer_rows[j], lines_at[y],
                    ).start()

    def combine(p):
        total = fwd_out[p, 0].astype(F32) + d_own[p, 0:toks, :]
        all_here(land2.at[p], part_sems.at[p, 9])
        for i in range(land2.shape[1]):
            total = total + land2[p, i].astype(F32)
        fin_out[p] = total.astype(BF16)
        pair_copy(p, fin_out, fin_in, 10).start()

    def finish():
        for p in range(parts):
            pair_copy(p, fin_out, fin_in, 10).wait_recv()
        for cols, ref in ((own, fin_out), (other, fin_in)):
            blocks = [ref[p].astype(F32) for p in range(parts)]
            whole = blocks[0] if parts == 1 else jnp.concatenate(blocks, axis=0)
            out_ref[:, cols] = whole.astype(BF16)

    route_table()
    for b in range(0, toks + PAIR, PAIR):
        attend(b)
    landed(proj_load[0])
    pl.semaphore_wait(barrier, len(steps) + 1)
    project(0)
    route_copies()
    if parts > 1:
        attend(toks + PAIR)
    spread_out(0)
    if parts > 1:
        for b in range(toks + 2 * PAIR, rows + PAIR, PAIR):
            attend(b)
        project(1)
        spread_out(1)
    issue(len(queue))
    all_here(w_in, w_sems.at[1])
    for p in range(parts):
        for j in range(req_count):
            table = w_own if j == 0 else w_in.at[j - 1]
            w_part[p, j * toks:(j + 1) * toks, :] = table[rows_of(p), :]
    for p in range(parts):
        collect(p)
        if p == 0:
            pltpu.make_async_copy(expert, expert, load_sems.at[7]).wait()
            pltpu.make_async_copy(shared_w, shared_w, load_sems.at[8]).wait()
        if ORD and p > 0:
            give_back(p - 1)
        experts(p)
        if not ORD or p == parts - 1:
            give_back(p)
    for p in range(parts):
        combine(p)
    finish()
    all_sent(w_in, w_sems.at[0])
    for p in range(parts):
        all_sent(land1.at[p], part_sems.at[p, 2])
        all_sent(land2.at[p], part_sems.at[p, 8])
        for src, dst, sem in (
            (pair1_out, pair1_in, 0), (fwd_out, fwd_in, 4), (pair2_out, pair2_in, 6),
            (fin_out, fin_in, 10),
        ):
            pair_copy(p, src, dst, sem).wait_send()


VMEM_SPEC = pl.BlockSpec(memory_space=pltpu.VMEM)
HBM_SPEC = pl.BlockSpec(memory_space=pltpu.HBM)


def per_device(
    req_count, head_count,
    hidden_in, queries, new_keys, new_values, key_cache, value_cache, lengths, out_proj,
    norm_gain, shared_gate, shared_up, shared_down, shared_score, expert_gate, expert_up,
    expert_down, expert_ids, route_weight,
):
    rows, model = hidden_in.shape
    span, width = key_cache.shape[1:]
    dma, vmem = pltpu.SemaphoreType.DMA, pltpu.VMEM
    parts, lines, half = PARTS, head_count // 2, model // 2
    toks = rows // parts
    tokens = req_count * toks
    return pl.pallas_call(
        functools.partial(layer_kernel, req_count, head_count),
        out_shape=pltpu.VMEM((rows, model), BF16),
        in_specs=[HBM_SPEC] * 18,
        out_specs=VMEM_SPEC,
        scratch_shapes=[
            pltpu.SMEM((rows,), jnp.int32),
            vmem((3, rows, width), BF16),
            vmem((rows, model), BF16),
            vmem((2, 1, model), F32),
            vmem(expert_ids.shape[::-1], jnp.int32),
            vmem(route_weight.shape[::-1], BF16),
            vmem((rows, span, width), BF16),
            vmem((rows, span, width), BF16),
            vmem(out_proj.shape, BF16),
            vmem((3,) + expert_down.shape[1:], BF16),
            vmem((3,) + shared_down.shape, BF16),
            dma((9,)), dma((rows // 2,)), dma((rows // 2,)),
            vmem((rows, width), F32),
            vmem((rows, 128), F32),
            vmem((req_count - 1, rows, 128), F32),
            vmem((parts, tokens, 128), F32),
            vmem((parts, tokens, half), F32),
            vmem((parts, tokens, half), F32),
            vmem((parts, tokens, half), F32),
            vmem((parts, toks, half), F32),
            vmem((parts, toks, half), F32),
            vmem((parts, toks, half), BF16),
            vmem((parts, req_count * lines - 1, toks, half), BF16),
            vmem((parts, req_count, toks, half), BF16),
            vmem((parts, req_count, toks, half), BF16),
            vmem((parts, tokens, half), BF16),
            vmem((parts, tokens, half), BF16),
            vmem((parts, req_count, toks, half), BF16),
            vmem((parts, req_count * lines - 1, toks, half), BF16),
            vmem((parts, toks, half), BF16),
            vmem((parts, toks, half), BF16),
            dma((2,)), dma((parts, 12)),
        ],
        compiler_params=pltpu.CompilerParams(
            vmem_limit_bytes=VM << 20, collective_id=0, has_side_effects=True
        ),
        name="layer",
    )(
        lengths, queries, new_keys, new_values, key_cache, value_cache, out_proj,
        hidden_in, norm_gain.reshape(1, model), shared_score.reshape(1, model),
        expert_ids.T, route_weight.T,
        shared_gate, shared_up, shared_down,
        jnp.swapaxes(expert_gate, 1, 2), jnp.swapaxes(expert_up, 1, 2), expert_down,
    )


def solution(mesh):
    in_specs = (
        P("req", None),
        P("req", "head"),
        P("req", "head"),
        P("req", "head"),
        P("req", None, "head"),
        P("req", None, "head"),
        P("req"),
        P("head", None),
        P(),
        P(("req", "head"), None),
        P(("req", "head"), None),
        P(("req", "head"), None),
        P(),
        P("req", None, "head"),
        P("req", None, "head"),
        P("req", "head", None),
        P("req", None),
        P("req", None),
    )
    body = functools.partial(per_device, mesh.shape["req"], mesh.shape["head"])
    return jax.shard_map(
        body, mesh=mesh, in_specs=in_specs, out_specs=P("req", None), check_vma=False
    )
```

```python
import functools

import jax
import jax.numpy as jnp
from jax import lax
from jax.experimental import pallas as pl
from jax.experimental.pallas import tpu as pltpu
from jax.sharding import PartitionSpec as P

PARTS = 2
AHEAD = 6
HD = 128
EPSILON = 1e-06
MESH = pl.DeviceIdType.MESH
BF16, F32 = jnp.bfloat16, jnp.float32
ROWS_BY_ROWS = (((1,), (1,)), ((), ()))


def silu(x):
    return x / (1.0 + jnp.exp(-x))


def layer_kernel(
    req_count, head_count,
    lengths_hbm, q_hbm, nk_hbm, nv_hbm, k_hbm, v_hbm, proj_hbm,
    hid_hbm, gain_hbm, score_hbm, ids_hbm, rw_hbm,
    sg_hbm, su_hbm, sd_hbm, eg_hbm, eu_hbm, ed_hbm,
    out_ref,
    lengths_ref, new_ref, hid_ref, gains, ids_ref, rw_ref,
    k_buf, v_buf, proj_buf, expert, shared_w, load_sems, k_sem, v_sem,
    attended, w_own, w_in, w_part, x_own, x_other, d_own,
    pair1_out, pair1_in, mine1, land1, fwd_out, fwd_in,
    pair2_out, pair2_in, send2, land2, fin_out, fin_in,
    w_sems, part_sems,
):
    rows, model = hid_ref.shape
    parts = mine1.shape[0]
    toks = rows // parts
    half = model // 2
    lines = head_count // 2
    me_r = lax.axis_index("req")
    me_h = lax.axis_index("head")
    me_y = lax.div(me_h, 2)
    me_c = lax.rem(me_h, 2)
    pair = me_y * 2 + 1 - me_c
    own = pl.ds(pl.multiple_of(me_c * half, 128), half)
    other = pl.ds(pl.multiple_of((1 - me_c) * half, 128), half)
    bits = []
    while (1 << len(bits)) < req_count:
        bits.append(lax.rem(lax.div(me_r, 1 << len(bits)), 2))

    def row(j):
        return sum(
            ((1 - bit) if (j >> i) & 1 else bit) * (1 << i) for i, bit in enumerate(bits)
        )

    peer_rows = [row(j) for j in range(req_count)]
    lines_at = [lax.rem(me_y + y, lines) * 2 + me_c for y in range(lines)]
    back_at = [lax.rem(me_y + lines - y, lines) * 2 + me_c for y in range(lines)]
    steps = [
        (j, y) for j in reversed(range(req_count)) for y in reversed(range(lines)) if j + y > 0
    ]

    def remote(src, dst, send, recv, r, h):
        return pltpu.make_async_remote_copy(
            src_ref=src, dst_ref=dst, send_sem=send, recv_sem=recv,
            device_id=(r, h), device_id_type=MESH,
        )

    def copies(sem, *pairs):
        return [pltpu.make_async_copy(src, dst, load_sems.at[sem]) for src, dst in pairs]

    new_loads = copies(0, (q_hbm, new_ref.at[0]), (nk_hbm, new_ref.at[1]), (nv_hbm, new_ref.at[2]))
    small = (
        copies(1, (lengths_hbm, lengths_ref)) + copies(2, (ids_hbm, ids_ref))
        + copies(3, (rw_hbm, rw_ref)) + copies(4, (hid_hbm, hid_ref))
    )
    gain_loads = copies(5, (gain_hbm, gains.at[0]), (score_hbm, gains.at[1]))
    proj_load = copies(6, (proj_hbm, proj_buf))
    expert_loads = copies(
        7, (eg_hbm.at[0], expert.at[0]), (eu_hbm.at[0], expert.at[1]), (ed_hbm.at[0], expert.at[2])
    )
    shared_loads = copies(
        8, (sg_hbm, shared_w.at[0]), (su_hbm, shared_w.at[1]), (sd_hbm, shared_w.at[2])
    )
    PAIR = 2

    def cache_load(hbm, buf, sem, b):
        rows_at = pl.ds(b, PAIR)
        return pltpu.make_async_copy(hbm.at[rows_at], buf.at[rows_at], sem.at[b // PAIR])

    k_load = [cache_load(k_hbm, k_buf, k_sem, b) for b in range(0, rows, PAIR)]
    v_load = [cache_load(v_hbm, v_buf, v_sem, b) for b in range(0, rows, PAIR)]
    queue = []
    for p in range(parts):
        pairs = range(p * toks // PAIR, (p + 1) * toks // PAIR)
        queue += [k_load[i] for i in pairs] + [v_load[i] for i in pairs]
        if p == 0:
            queue += proj_load
    queue += expert_loads + shared_loads
    issued = [0]

    def issue(upto):
        while issued[0] < min(upto, len(queue)):
            queue[issued[0]].start()
            issued[0] += 1

    def landed(copy):
        copy.wait()
        issue(next(i for i, c in enumerate(queue) if c is copy) + 1 + AHEAD)

    for load in new_loads + small + gain_loads:
        load.start()
    issue(AHEAD)
    barrier = pltpu.get_barrier_semaphore()
    for j, y in steps:
        pl.semaphore_signal(
            barrier, inc=1, device_id=(peer_rows[j], back_at[y]), device_id_type=MESH
        )
    pl.semaphore_signal(barrier, inc=1, device_id=(me_r, pair), device_id_type=MESH)

    pltpu.make_async_copy(new_ref, new_ref, load_sems.at[0]).wait()
    for load in small:
        load.wait()
    pltpu.make_async_copy(gains, gains, load_sems.at[5]).wait()

    span, width = k_buf.shape[1:]
    scale = HD ** (-0.5)
    group = max(8, width // HD)
    own_head = (
        lax.broadcasted_iota(jnp.int32, (group, width), 0)
        == lax.broadcasted_iota(jnp.int32, (group, width), 1) // HD
    )
    position = lax.broadcasted_iota(jnp.int32, (group, span), 1)
    queries = new_ref[0].astype(F32)
    own_keys = new_ref[1].astype(F32)
    own_values = new_ref[2].astype(F32)

    def score(b):
        spread = jnp.where(own_head, queries[b:b + 1, :], 0.0)
        scores = lax.dot_general(
            spread.astype(BF16), k_buf[b], ROWS_BY_ROWS, preferred_element_type=F32
        )
        own_score = jnp.sum(spread * own_keys[b:b + 1, :], axis=1, keepdims=True)
        scores = jnp.where(position < lengths_ref[b], scores, -1e30)
        highest = jnp.maximum(jnp.max(scores, axis=1, keepdims=True), own_score)
        exps = jnp.exp((scores - highest) * scale)
        own_exp = jnp.exp((own_score - highest) * scale)
        share = 1.0 / (jnp.sum(exps, axis=1, keepdims=True) + own_exp)
        own_part = jnp.sum(
            jnp.where(own_head, own_exp * own_values[b:b + 1, :], 0.0) * share,
            axis=0, keepdims=True,
        )
        return exps.astype(BF16), share, own_part

    def mix(b, scored):
        exps, share, own_part = scored
        mixed = jnp.dot(exps, v_buf[b], preferred_element_type=F32)
        mixed = jnp.where(own_head, mixed * share, 0.0)
        attended[b:b + 1, :] = jnp.sum(mixed, axis=0, keepdims=True) + own_part

    scored = {}

    def attend(score_pair, mix_pair):
        if score_pair is not None:
            landed(k_load[score_pair])
        if mix_pair is not None:
            landed(v_load[mix_pair])
        for i in range(PAIR):
            if score_pair is not None:
                b = score_pair * PAIR + i
                scored[b] = score(b)
            if mix_pair is not None:
                b = mix_pair * PAIR + i
                mix(b, scored.pop(b))

    def route_table():
        lane = lax.broadcasted_iota(jnp.int32, (rows, 128), 1).astype(F32)
        table = jnp.zeros((rows, 128), F32)
        route = rw_ref[...].astype(F32)
        ids = ids_ref[...].astype(F32)
        diagonal = (
            lax.broadcasted_iota(jnp.int32, (rows, rows), 0)
            == lax.broadcasted_iota(jnp.int32, (rows, rows), 1)
        )
        for k in range(ids.shape[0]):
            chosen = jnp.sum(jnp.where(diagonal, ids[k:k + 1, :], 0.0), axis=1, keepdims=True)
            share = jnp.sum(jnp.where(diagonal, route[k:k + 1, :], 0.0), axis=1, keepdims=True)
            table = table + jnp.where(chosen == lane, share, 0.0)
        w_own[...] = table

    def route_copies():
        for j in reversed(range(1, req_count)):
            remote(w_own, w_in.at[j - 1], w_sems.at[0], w_sems.at[1], peer_rows[j], me_h).start()

    def all_sent(ref, sem):
        remote(ref, ref, sem, sem, me_r, pair).wait_send()

    def all_here(ref, sem):
        remote(ref, ref, sem, sem, me_r, pair).wait_recv()

    def rows_of(p):
        return slice(p * toks, (p + 1) * toks)

    def pair_copy(p, src, dst, sem):
        return remote(
            src.at[p], dst.at[p], part_sems.at[p, sem], part_sems.at[p, sem + 1], me_r, pair
        )

    kept = {}

    def project(p):
        mixed = attended[rows_of(p), :].astype(BF16)
        pair1_out[p] = jnp.dot(mixed, proj_buf[:, other], preferred_element_type=F32)
        pair_copy(p, pair1_out, pair1_in, 0).start()
        hidden = jnp.where(me_y == 0, hid_ref[:, own].astype(F32), 0.0)
        kept[p] = (
            jnp.dot(mixed, proj_buf[:, own], preferred_element_type=F32) + hidden[rows_of(p)]
        )

    def spread_out(p):
        pair_copy(p, pair1_out, pair1_in, 0).wait_recv()
        mine1[p] = (kept.pop(p) + pair1_in[p]).astype(BF16)
        for j, y in reversed(steps):
            remote(
                mine1.at[p], land1.at[p, j * lines + y - 1], part_sems.at[p, 2],
                part_sems.at[p, 3], peer_rows[j], lines_at[y],
            ).start()

    def collect(p):
        all_here(land1.at[p], part_sems.at[p, 3])
        for j in range(req_count):
            total = None
            for y in range(lines):
                block = land1[p, j * lines + y - 1] if j + y > 0 else mine1[p]
                block = block.astype(F32)
                total = block if total is None else total + block
            resid = total.astype(BF16)
            fwd_out[p, j] = resid
            x_own[p, j * toks:(j + 1) * toks, :] = resid.astype(F32)
        pair_copy(p, fwd_out, fwd_in, 4).start()

    def half_terms(x, cols):
        square = jnp.sum(x * x, axis=1, keepdims=True)
        gained = (x * gains[0, :, cols]).astype(BF16)
        logit = jnp.sum(gained.astype(F32) * gains[1, :, cols], axis=1, keepdims=True)
        return [square, logit] + [
            lax.dot_general(gained, w[i, :, cols], ROWS_BY_ROWS, preferred_element_type=F32)
            for w in (expert, shared_w) for i in range(2)
        ]

    def experts(p):
        first = half_terms(x_own[p], own)
        if p > 0:
            give_back(p - 1)
        pair_copy(p, fwd_out, fwd_in, 4).wait_recv()
        for j in range(req_count):
            x_other[p, j * toks:(j + 1) * toks, :] = fwd_in[p, j].astype(F32)
        second = half_terms(x_other[p], other)
        square, logit, g, u, shared_g, shared_u = [a + b for a, b in zip(first, second)]
        inverse = lax.rsqrt(square / model + EPSILON)
        gate_scale = 1.0 / (1.0 + jnp.exp(-logit * inverse))
        lane = lax.broadcasted_iota(jnp.int32, w_part.shape[1:], 1)
        weight = jnp.sum(jnp.where(lane == me_r, w_part[p], 0.0), axis=1, keepdims=True)
        inner = (silu(g * inverse) * (u * (inverse * weight))).astype(BF16)
        hidden = (silu(shared_g * inverse) * (shared_u * (inverse * gate_scale))).astype(BF16)

        def down(cols):
            return (
                jnp.dot(inner, expert[2, :, cols], preferred_element_type=F32)
                + jnp.dot(hidden, shared_w[2, :, cols], preferred_element_type=F32)
            )

        pair2_out[p] = down(other).astype(BF16)
        pair_copy(p, pair2_out, pair2_in, 6).start()
        d_own[p] = down(own)

    def give_back(p):
        pair_copy(p, pair2_out, pair2_in, 6).wait_recv()
        d_own[p] = d_own[p] + pair2_in[p].astype(F32)
        for j in reversed(range(req_count)):
            send2[p, j] = d_own[p, j * toks:(j + 1) * toks, :].astype(BF16)
            for y in reversed(range(lines)):
                if j + y > 0:
                    remote(
                        send2.at[p, j], land2.at[p, j * lines + y - 1], part_sems.at[p, 8],
                        part_sems.at[p, 9], peer_rows[j], lines_at[y],
                    ).start()

    def combine(p):
        total = fwd_out[p, 0].astype(F32) + d_own[p, 0:toks, :]
        all_here(land2.at[p], part_sems.at[p, 9])
        for i in range(land2.shape[1]):
            total = total + land2[p, i].astype(F32)
        fin_out[p] = total.astype(BF16)
        pair_copy(p, fin_out, fin_in, 10).start()

    def finish():
        for p in range(parts):
            pair_copy(p, fin_out, fin_in, 10).wait_recv()
        for cols, ref in ((own, fin_out), (other, fin_in)):
            blocks = [ref[p].astype(F32) for p in range(parts)]
            whole = blocks[0] if parts == 1 else jnp.concatenate(blocks, axis=0)
            out_ref[:, cols] = whole.astype(BF16)

    route_table()
    for p in range(parts):
        first, last = p * toks // PAIR, (p + 1) * toks // PAIR - 1
        attend(first, None)
        if p > 0:
            spread_out(p - 1)
        for i in range(first, last):
            attend(i + 1, i)
        attend(None, last)
        if p == 0:
            landed(proj_load[0])
            pl.semaphore_wait(barrier, len(steps) + 1)
        project(p)
        if p == 0:
            route_copies()
    spread_out(parts - 1)
    issue(len(queue))
    all_here(w_in, w_sems.at[1])
    for p in range(parts):
        for j in range(req_count):
            table = w_own if j == 0 else w_in.at[j - 1]
            w_part[p, j * toks:(j + 1) * toks, :] = table[rows_of(p), :]
    for p in range(parts):
        collect(p)
        if p == 0:
            pltpu.make_async_copy(expert, expert, load_sems.at[7]).wait()
            pltpu.make_async_copy(shared_w, shared_w, load_sems.at[8]).wait()
        experts(p)
    give_back(parts - 1)
    for p in range(parts):
        combine(p)
    finish()
    all_sent(w_in, w_sems.at[0])
    for p in range(parts):
        all_sent(land1.at[p], part_sems.at[p, 2])
        all_sent(land2.at[p], part_sems.at[p, 8])
        for src, dst, sem in (
            (pair1_out, pair1_in, 0), (fwd_out, fwd_in, 4), (pair2_out, pair2_in, 6),
            (fin_out, fin_in, 10),
        ):
            pair_copy(p, src, dst, sem).wait_send()


VMEM_SPEC = pl.BlockSpec(memory_space=pltpu.VMEM)
HBM_SPEC = pl.BlockSpec(memory_space=pltpu.HBM)


def per_device(
    req_count, head_count,
    hidden_in, queries, new_keys, new_values, key_cache, value_cache, lengths, out_proj,
    norm_gain, shared_gate, shared_up, shared_down, shared_score, expert_gate, expert_up,
    expert_down, expert_ids, route_weight,
):
    rows, model = hidden_in.shape
    span, width = key_cache.shape[1:]
    dma, vmem = pltpu.SemaphoreType.DMA, pltpu.VMEM
    parts, lines, half = PARTS, head_count // 2, model // 2
    toks = rows // parts
    tokens = req_count * toks
    return pl.pallas_call(
        functools.partial(layer_kernel, req_count, head_count),
        out_shape=pltpu.VMEM((rows, model), BF16),
        in_specs=[HBM_SPEC] * 18,
        out_specs=VMEM_SPEC,
        scratch_shapes=[
            pltpu.SMEM((rows,), jnp.int32),
            vmem((3, rows, width), BF16),
            vmem((rows, model), BF16),
            vmem((2, 1, model), F32),
            vmem(expert_ids.shape[::-1], jnp.int32),
            vmem(route_weight.shape[::-1], BF16),
            vmem((rows, span, width), BF16),
            vmem((rows, span, width), BF16),
            vmem(out_proj.shape, BF16),
            vmem((3,) + expert_down.shape[1:], BF16),
            vmem((3,) + shared_down.shape, BF16),
            dma((9,)), dma((rows // 2,)), dma((rows // 2,)),
            vmem((rows, width), F32),
            vmem((rows, 128), F32),
            vmem((req_count - 1, rows, 128), F32),
            vmem((parts, tokens, 128), F32),
            vmem((parts, tokens, half), F32),
            vmem((parts, tokens, half), F32),
            vmem((parts, tokens, half), F32),
            vmem((parts, toks, half), F32),
            vmem((parts, toks, half), F32),
            vmem((parts, toks, half), BF16),
            vmem((parts, req_count * lines - 1, toks, half), BF16),
            vmem((parts, req_count, toks, half), BF16),
            vmem((parts, req_count, toks, half), BF16),
            vmem((parts, tokens, half), BF16),
            vmem((parts, tokens, half), BF16),
            vmem((parts, req_count, toks, half), BF16),
            vmem((parts, req_count * lines - 1, toks, half), BF16),
            vmem((parts, toks, half), BF16),
            vmem((parts, toks, half), BF16),
            dma((2,)), dma((parts, 12)),
        ],
        compiler_params=pltpu.CompilerParams(
            vmem_limit_bytes=63 << 20, collective_id=0, has_side_effects=True
        ),
        name="layer",
    )(
        lengths, queries, new_keys, new_values, key_cache, value_cache, out_proj,
        hidden_in, norm_gain.reshape(1, model), shared_score.reshape(1, model),
        expert_ids.T, route_weight.T,
        shared_gate, shared_up, shared_down,
        jnp.swapaxes(expert_gate, 1, 2), jnp.swapaxes(expert_up, 1, 2), expert_down,
    )


def solution(mesh):
    in_specs = (
        P("req", None),
        P("req", "head"),
        P("req", "head"),
        P("req", "head"),
        P("req", None, "head"),
        P("req", None, "head"),
        P("req"),
        P("head", None),
        P(),
        P(("req", "head"), None),
        P(("req", "head"), None),
        P(("req", "head"), None),
        P(),
        P("req", None, "head"),
        P("req", None, "head"),
        P("req", "head", None),
        P("req", None),
        P("req", None),
    )
    body = functools.partial(per_device, mesh.shape["req"], mesh.shape["head"])
    return jax.shard_map(
        body, mesh=mesh, in_specs=in_specs, out_specs=P("req", None), check_vma=False
    )
```

```python
import functools

import jax
import jax.numpy as jnp
from jax import lax
from jax.experimental import pallas as pl
from jax.experimental.pallas import tpu as pltpu
from jax.sharding import PartitionSpec as P

PARTS = 2
AHEAD = 6
HD = 128
EPSILON = 1e-06
MESH = pl.DeviceIdType.MESH
BF16, F32 = jnp.bfloat16, jnp.float32
ROWS_BY_ROWS = (((1,), (1,)), ((), ()))


def silu(x):
    return x / (1.0 + jnp.exp(-x))


def layer_kernel(
    req_count, head_count,
    lengths_hbm, q_hbm, nk_hbm, nv_hbm, k_hbm, v_hbm, proj_hbm,
    hid_hbm, gain_hbm, score_hbm, ids_hbm, rw_hbm,
    sg_hbm, su_hbm, sd_hbm, eg_hbm, eu_hbm, ed_hbm,
    out_ref,
    lengths_ref, new_ref, hid_ref, gains, ids_ref, rw_ref,
    k_buf, v_buf, proj_buf, expert, shared_w, load_sems, k_sem, v_sem,
    attended, w_own, w_in, w_part, x_own, x_other, d_own,
    pair1_out, pair1_in, mine1, land1, fwd_out, fwd_in,
    pair2_out, pair2_in, send2, land2, fin_out, fin_in,
    w_sems, part_sems,
):
    rows, model = hid_ref.shape
    parts = mine1.shape[0]
    toks = rows // parts
    half = model // 2
    lines = head_count // 2
    me_r = lax.axis_index("req")
    me_h = lax.axis_index("head")
    me_y = lax.div(me_h, 2)
    me_c = lax.rem(me_h, 2)
    pair = me_y * 2 + 1 - me_c
    own = pl.ds(pl.multiple_of(me_c * half, 128), half)
    other = pl.ds(pl.multiple_of((1 - me_c) * half, 128), half)
    bits = []
    while (1 << len(bits)) < req_count:
        bits.append(lax.rem(lax.div(me_r, 1 << len(bits)), 2))

    def row(j):
        return sum(
            ((1 - bit) if (j >> i) & 1 else bit) * (1 << i) for i, bit in enumerate(bits)
        )

    peer_rows = [row(j) for j in range(req_count)]
    lines_at = [lax.rem(me_y + y, lines) * 2 + me_c for y in range(lines)]
    back_at = [lax.rem(me_y + lines - y, lines) * 2 + me_c for y in range(lines)]
    steps = [
        (j, y) for j in reversed(range(req_count)) for y in reversed(range(lines)) if j + y > 0
    ]

    targets = []
    me_chip = me_r * lines + me_y
    for k in range(req_count * lines - 1):
        chip = k + jnp.where(me_chip <= k, 1, 0)
        r, y = lax.div(chip, lines), lax.rem(chip, lines)
        j = 0
        for i, bit in enumerate(bits):
            away = lax.rem(lax.div(r, 1 << i), 2)
            j = j + (away + bit - 2 * away * bit) * (1 << i)
        slot = j * lines + lax.rem(y + lines - me_y, lines) - 1
        targets.append((r, y * 2 + me_c, j, slot))

    def remote(src, dst, send, recv, r, h):
        return pltpu.make_async_remote_copy(
            src_ref=src, dst_ref=dst, send_sem=send, recv_sem=recv,
            device_id=(r, h), device_id_type=MESH,
        )

    def copies(sem, *pairs):
        return [pltpu.make_async_copy(src, dst, load_sems.at[sem]) for src, dst in pairs]

    new_loads = copies(0, (q_hbm, new_ref.at[0]), (nk_hbm, new_ref.at[1]), (nv_hbm, new_ref.at[2]))
    small = (
        copies(1, (lengths_hbm, lengths_ref)) + copies(2, (ids_hbm, ids_ref))
        + copies(3, (rw_hbm, rw_ref)) + copies(4, (hid_hbm, hid_ref))
    )
    gain_loads = copies(5, (gain_hbm, gains.at[0]), (score_hbm, gains.at[1]))
    proj_load = copies(6, (proj_hbm, proj_buf))
    expert_loads = copies(
        7, (eg_hbm.at[0], expert.at[0]), (eu_hbm.at[0], expert.at[1]), (ed_hbm.at[0], expert.at[2])
    )
    shared_loads = copies(
        8, (sg_hbm, shared_w.at[0]), (su_hbm, shared_w.at[1]), (sd_hbm, shared_w.at[2])
    )
    PAIR = 2

    def cache_load(hbm, buf, sem, b):
        rows_at = pl.ds(b, PAIR)
        return pltpu.make_async_copy(hbm.at[rows_at], buf.at[rows_at], sem.at[b // PAIR])

    k_load = [cache_load(k_hbm, k_buf, k_sem, b) for b in range(0, rows, PAIR)]
    v_load = [cache_load(v_hbm, v_buf, v_sem, b) for b in range(0, rows, PAIR)]
    queue = []
    for p in range(parts):
        pairs = range(p * toks // PAIR, (p + 1) * toks // PAIR)
        queue += [k_load[i] for i in pairs] + [v_load[i] for i in pairs]
        if p == 0:
            queue += proj_load
    queue += expert_loads + shared_loads
    issued = [0]

    def issue(upto):
        while issued[0] < min(upto, len(queue)):
            queue[issued[0]].start()
            issued[0] += 1

    def landed(copy):
        copy.wait()
        issue(next(i for i, c in enumerate(queue) if c is copy) + 1 + AHEAD)

    for load in new_loads + small + gain_loads:
        load.start()
    issue(AHEAD)
    barrier = pltpu.get_barrier_semaphore()
    for j, y in steps:
        pl.semaphore_signal(
            barrier, inc=1, device_id=(peer_rows[j], back_at[y]), device_id_type=MESH
        )
    pl.semaphore_signal(barrier, inc=1, device_id=(me_r, pair), device_id_type=MESH)

    pltpu.make_async_copy(new_ref, new_ref, load_sems.at[0]).wait()
    for load in small:
        load.wait()
    pltpu.make_async_copy(gains, gains, load_sems.at[5]).wait()

    span, width = k_buf.shape[1:]
    scale = HD ** (-0.5)
    group = max(8, width // HD)
    own_head = (
        lax.broadcasted_iota(jnp.int32, (group, width), 0)
        == lax.broadcasted_iota(jnp.int32, (group, width), 1) // HD
    )
    position = lax.broadcasted_iota(jnp.int32, (group, span), 1)
    queries = new_ref[0].astype(F32)
    own_keys = new_ref[1].astype(F32)
    own_values = new_ref[2].astype(F32)

    def score(b):
        spread = jnp.where(own_head, queries[b:b + 1, :], 0.0)
        scores = lax.dot_general(
            spread.astype(BF16), k_buf[b], ROWS_BY_ROWS, preferred_element_type=F32
        )
        own_score = jnp.sum(spread * own_keys[b:b + 1, :], axis=1, keepdims=True)
        scores = jnp.where(position < lengths_ref[b], scores, -1e30)
        highest = jnp.maximum(jnp.max(scores, axis=1, keepdims=True), own_score)
        exps = jnp.exp((scores - highest) * scale)
        own_exp = jnp.exp((own_score - highest) * scale)
        share = 1.0 / (jnp.sum(exps, axis=1, keepdims=True) + own_exp)
        own_part = jnp.sum(
            jnp.where(own_head, own_exp * own_values[b:b + 1, :], 0.0) * share,
            axis=0, keepdims=True,
        )
        return exps.astype(BF16), share, own_part

    def mix(b, scored):
        exps, share, own_part = scored
        mixed = jnp.dot(exps, v_buf[b], preferred_element_type=F32)
        mixed = jnp.where(own_head, mixed * share, 0.0)
        attended[b:b + 1, :] = jnp.sum(mixed, axis=0, keepdims=True) + own_part

    scored = {}

    def attend(score_pair, mix_pair):
        if score_pair is not None:
            landed(k_load[score_pair])
        if mix_pair is not None:
            landed(v_load[mix_pair])
        for i in range(PAIR):
            if score_pair is not None:
                b = score_pair * PAIR + i
                scored[b] = score(b)
            if mix_pair is not None:
                b = mix_pair * PAIR + i
                mix(b, scored.pop(b))

    def route_table():
        lane = lax.broadcasted_iota(jnp.int32, (rows, 128), 1).astype(F32)
        table = jnp.zeros((rows, 128), F32)
        route = rw_ref[...].astype(F32)
        ids = ids_ref[...].astype(F32)
        diagonal = (
            lax.broadcasted_iota(jnp.int32, (rows, rows), 0)
            == lax.broadcasted_iota(jnp.int32, (rows, rows), 1)
        )
        for k in range(ids.shape[0]):
            chosen = jnp.sum(jnp.where(diagonal, ids[k:k + 1, :], 0.0), axis=1, keepdims=True)
            share = jnp.sum(jnp.where(diagonal, route[k:k + 1, :], 0.0), axis=1, keepdims=True)
            table = table + jnp.where(chosen == lane, share, 0.0)
        w_own[...] = table

    def route_copies():
        for j in reversed(range(1, req_count)):
            remote(w_own, w_in.at[j - 1], w_sems.at[0], w_sems.at[1], peer_rows[j], me_h).start()

    def all_sent(ref, sem):
        remote(ref, ref, sem, sem, me_r, pair).wait_send()

    def all_here(ref, sem):
        remote(ref, ref, sem, sem, me_r, pair).wait_recv()

    def rows_of(p):
        return slice(p * toks, (p + 1) * toks)

    def pair_copy(p, src, dst, sem):
        return remote(
            src.at[p], dst.at[p], part_sems.at[p, sem], part_sems.at[p, sem + 1], me_r, pair
        )

    kept = {}

    def project(p):
        mixed = attended[rows_of(p), :].astype(BF16)
        pair1_out[p] = jnp.dot(mixed, proj_buf[:, other], preferred_element_type=F32)
        pair_copy(p, pair1_out, pair1_in, 0).start()
        hidden = jnp.where(me_y == 0, hid_ref[:, own].astype(F32), 0.0)
        kept[p] = (
            jnp.dot(mixed, proj_buf[:, own], preferred_element_type=F32) + hidden[rows_of(p)]
        )

    def spread_out(p):
        pair_copy(p, pair1_out, pair1_in, 0).wait_recv()
        mine1[p] = (kept.pop(p) + pair1_in[p]).astype(BF16)
        for j, y in reversed(steps):
            remote(
                mine1.at[p], land1.at[p, j * lines + y - 1], part_sems.at[p, 2],
                part_sems.at[p, 3], peer_rows[j], lines_at[y],
            ).start()

    def collect(p):
        all_here(land1.at[p], part_sems.at[p, 3])
        for j in range(req_count):
            total = None
            for y in range(lines):
                block = land1[p, j * lines + y - 1] if j + y > 0 else mine1[p]
                block = block.astype(F32)
                total = block if total is None else total + block
            resid = total.astype(BF16)
            fwd_out[p, j] = resid
            x_own[p, j * toks:(j + 1) * toks, :] = resid.astype(F32)
        pair_copy(p, fwd_out, fwd_in, 4).start()

    def half_terms(x, cols):
        square = jnp.sum(x * x, axis=1, keepdims=True)
        gained = (x * gains[0, :, cols]).astype(BF16)
        logit = jnp.sum(gained.astype(F32) * gains[1, :, cols], axis=1, keepdims=True)
        return [square, logit] + [
            lax.dot_general(gained, w[i, :, cols], ROWS_BY_ROWS, preferred_element_type=F32)
            for w in (expert, shared_w) for i in range(2)
        ]

    def experts(p):
        first = half_terms(x_own[p], own)
        if p > 0:
            give_back(p - 1)
        pair_copy(p, fwd_out, fwd_in, 4).wait_recv()
        for j in range(req_count):
            x_other[p, j * toks:(j + 1) * toks, :] = fwd_in[p, j].astype(F32)
        second = half_terms(x_other[p], other)
        square, logit, g, u, shared_g, shared_u = [a + b for a, b in zip(first, second)]
        inverse = lax.rsqrt(square / model + EPSILON)
        gate_scale = 1.0 / (1.0 + jnp.exp(-logit * inverse))
        lane = lax.broadcasted_iota(jnp.int32, w_part.shape[1:], 1)
        weight = jnp.sum(jnp.where(lane == me_r, w_part[p], 0.0), axis=1, keepdims=True)
        inner = (silu(g * inverse) * (u * (inverse * weight))).astype(BF16)
        hidden = (silu(shared_g * inverse) * (shared_u * (inverse * gate_scale))).astype(BF16)

        def down(cols):
            return (
                jnp.dot(inner, expert[2, :, cols], preferred_element_type=F32)
                + jnp.dot(hidden, shared_w[2, :, cols], preferred_element_type=F32)
            )

        pair2_out[p] = down(other).astype(BF16)
        pair_copy(p, pair2_out, pair2_in, 6).start()
        d_own[p] = down(own)

    def give_back(p):
        pair_copy(p, pair2_out, pair2_in, 6).wait_recv()
        d_own[p] = d_own[p] + pair2_in[p].astype(F32)
        for j in range(req_count):
            send2[p, j] = d_own[p, j * toks:(j + 1) * toks, :].astype(BF16)
        for r, h, j, slot in targets:
            remote(
                send2.at[p, j], land2.at[p, slot], part_sems.at[p, 8], part_sems.at[p, 9], r, h
            ).start()

    def combine(p):
        total = fwd_out[p, 0].astype(F32) + d_own[p, 0:toks, :]
        all_here(land2.at[p], part_sems.at[p, 9])
        for i in range(land2.shape[1]):
            total = total + land2[p, i].astype(F32)
        fin_out[p] = total.astype(BF16)
        pair_copy(p, fin_out, fin_in, 10).start()

    def finish():
        for p in range(parts):
            pair_copy(p, fin_out, fin_in, 10).wait_recv()
        for cols, ref in ((own, fin_out), (other, fin_in)):
            blocks = [ref[p].astype(F32) for p in range(parts)]
            whole = blocks[0] if parts == 1 else jnp.concatenate(blocks, axis=0)
            out_ref[:, cols] = whole.astype(BF16)

    route_table()
    for p in range(parts):
        first, last = p * toks // PAIR, (p + 1) * toks // PAIR - 1
        attend(first, None)
        if p > 0:
            spread_out(p - 1)
        for i in range(first, last):
            attend(i + 1, i)
        attend(None, last)
        if p == 0:
            landed(proj_load[0])
            pl.semaphore_wait(barrier, len(steps) + 1)
        project(p)
        if p == 0:
            route_copies()
    spread_out(parts - 1)
    issue(len(queue))
    all_here(w_in, w_sems.at[1])
    for p in range(parts):
        for j in range(req_count):
            table = w_own if j == 0 else w_in.at[j - 1]
            w_part[p, j * toks:(j + 1) * toks, :] = table[rows_of(p), :]
    for p in range(parts):
        collect(p)
        if p == 0:
            pltpu.make_async_copy(expert, expert, load_sems.at[7]).wait()
            pltpu.make_async_copy(shared_w, shared_w, load_sems.at[8]).wait()
        experts(p)
    give_back(parts - 1)
    for p in range(parts):
        combine(p)
    finish()
    all_sent(w_in, w_sems.at[0])
    for p in range(parts):
        all_sent(land1.at[p], part_sems.at[p, 2])
        all_sent(land2.at[p], part_sems.at[p, 8])
        for src, dst, sem in (
            (pair1_out, pair1_in, 0), (fwd_out, fwd_in, 4), (pair2_out, pair2_in, 6),
            (fin_out, fin_in, 10),
        ):
            pair_copy(p, src, dst, sem).wait_send()


VMEM_SPEC = pl.BlockSpec(memory_space=pltpu.VMEM)
HBM_SPEC = pl.BlockSpec(memory_space=pltpu.HBM)


def per_device(
    req_count, head_count,
    hidden_in, queries, new_keys, new_values, key_cache, value_cache, lengths, out_proj,
    norm_gain, shared_gate, shared_up, shared_down, shared_score, expert_gate, expert_up,
    expert_down, expert_ids, route_weight,
):
    rows, model = hidden_in.shape
    span, width = key_cache.shape[1:]
    dma, vmem = pltpu.SemaphoreType.DMA, pltpu.VMEM
    parts, lines, half = PARTS, head_count // 2, model // 2
    toks = rows // parts
    tokens = req_count * toks
    return pl.pallas_call(
        functools.partial(layer_kernel, req_count, head_count),
        out_shape=pltpu.VMEM((rows, model), BF16),
        in_specs=[HBM_SPEC] * 18,
        out_specs=VMEM_SPEC,
        scratch_shapes=[
            pltpu.SMEM((rows,), jnp.int32),
            vmem((3, rows, width), BF16),
            vmem((rows, model), BF16),
            vmem((2, 1, model), F32),
            vmem(expert_ids.shape[::-1], jnp.int32),
            vmem(route_weight.shape[::-1], BF16),
            vmem((rows, span, width), BF16),
            vmem((rows, span, width), BF16),
            vmem(out_proj.shape, BF16),
            vmem((3,) + expert_down.shape[1:], BF16),
            vmem((3,) + shared_down.shape, BF16),
            dma((9,)), dma((rows // 2,)), dma((rows // 2,)),
            vmem((rows, width), F32),
            vmem((rows, 128), F32),
            vmem((req_count - 1, rows, 128), F32),
            vmem((parts, tokens, 128), F32),
            vmem((parts, tokens, half), F32),
            vmem((parts, tokens, half), F32),
            vmem((parts, tokens, half), F32),
            vmem((parts, toks, half), F32),
            vmem((parts, toks, half), F32),
            vmem((parts, toks, half), BF16),
            vmem((parts, req_count * lines - 1, toks, half), BF16),
            vmem((parts, req_count, toks, half), BF16),
            vmem((parts, req_count, toks, half), BF16),
            vmem((parts, tokens, half), BF16),
            vmem((parts, tokens, half), BF16),
            vmem((parts, req_count, toks, half), BF16),
            vmem((parts, req_count * lines - 1, toks, half), BF16),
            vmem((parts, toks, half), BF16),
            vmem((parts, toks, half), BF16),
            dma((2,)), dma((parts, 12)),
        ],
        compiler_params=pltpu.CompilerParams(
            vmem_limit_bytes=63 << 20, collective_id=0, has_side_effects=True
        ),
        name="layer",
    )(
        lengths, queries, new_keys, new_values, key_cache, value_cache, out_proj,
        hidden_in, norm_gain.reshape(1, model), shared_score.reshape(1, model),
        expert_ids.T, route_weight.T,
        shared_gate, shared_up, shared_down,
        jnp.swapaxes(expert_gate, 1, 2), jnp.swapaxes(expert_up, 1, 2), expert_down,
    )


def solution(mesh):
    in_specs = (
        P("req", None),
        P("req", "head"),
        P("req", "head"),
        P("req", "head"),
        P("req", None, "head"),
        P("req", None, "head"),
        P("req"),
        P("head", None),
        P(),
        P(("req", "head"), None),
        P(("req", "head"), None),
        P(("req", "head"), None),
        P(),
        P("req", None, "head"),
        P("req", None, "head"),
        P("req", "head", None),
        P("req", None),
        P("req", None),
    )
    body = functools.partial(per_device, mesh.shape["req"], mesh.shape["head"])
    return jax.shard_map(
        body, mesh=mesh, in_specs=in_specs, out_specs=P("req", None), check_vma=False
    )
```

```python
import functools

import jax
import jax.numpy as jnp
from jax import lax
from jax.experimental import pallas as pl
from jax.experimental.pallas import tpu as pltpu
from jax.sharding import PartitionSpec as P

PARTS = 2
AHEAD = 6
HD = 128
EPSILON = 1e-06
MESH = pl.DeviceIdType.MESH
BF16, F32 = jnp.bfloat16, jnp.float32
ROWS_BY_ROWS = (((1,), (1,)), ((), ()))


def silu(x):
    return x / (1.0 + jnp.exp(-x))


def layer_kernel(
    req_count, head_count,
    lengths_hbm, q_hbm, nk_hbm, nv_hbm, k_hbm, v_hbm, proj_hbm,
    hid_hbm, gain_hbm, score_hbm, ids_hbm, rw_hbm,
    sg_hbm, su_hbm, sd_hbm, eg_hbm, eu_hbm, ed_hbm,
    out_ref,
    lengths_ref, new_ref, hid_ref, gains, ids_ref, rw_ref,
    k_buf, v_buf, proj_buf, expert, shared_w, load_sems, k_sem, v_sem,
    attended, w_own, w_in, w_part, x_own, x_other, d_own,
    pair1_out, pair1_in, mine1, land1, fwd_out, fwd_in,
    pair2_out, pair2_in, send2, land2, fin_out, fin_in,
    tally, w_sems, part_sems, send_sem,
):
    rows, model = hid_ref.shape
    parts = mine1.shape[0]
    toks = rows // parts
    half = model // 2
    lines = head_count // 2
    me_r = lax.axis_index("req")
    me_h = lax.axis_index("head")
    me_y = lax.div(me_h, 2)
    me_c = lax.rem(me_h, 2)
    pair = me_y * 2 + 1 - me_c
    own = pl.ds(pl.multiple_of(me_c * half, 128), half)
    other = pl.ds(pl.multiple_of((1 - me_c) * half, 128), half)
    bits = []
    while (1 << len(bits)) < req_count:
        bits.append(lax.rem(lax.div(me_r, 1 << len(bits)), 2))

    def row(j):
        return sum(
            ((1 - bit) if (j >> i) & 1 else bit) * (1 << i) for i, bit in enumerate(bits)
        )

    peer_rows = [row(j) for j in range(req_count)]
    lines_at = [lax.rem(me_y + y, lines) * 2 + me_c for y in range(lines)]
    back_at = [lax.rem(me_y + lines - y, lines) * 2 + me_c for y in range(lines)]
    steps = [
        (j, y) for j in reversed(range(req_count)) for y in reversed(range(lines)) if j + y > 0
    ]

    targets = []
    me_chip = me_r * lines + me_y
    for k in range(req_count * lines - 1):
        chip = k + jnp.where(me_chip <= k, 1, 0)
        r, y = lax.div(chip, lines), lax.rem(chip, lines)
        j = 0
        for i, bit in enumerate(bits):
            away = lax.rem(lax.div(r, 1 << i), 2)
            j = j + (away + bit - 2 * away * bit) * (1 << i)
        slot = j * lines + lax.rem(y + lines - me_y, lines) - 1
        targets.append((r, y * 2 + me_c, j, slot))

    def remote(src, dst, send, recv, r, h):
        return pltpu.make_async_remote_copy(
            src_ref=src, dst_ref=dst, send_sem=send, recv_sem=recv,
            device_id=(r, h), device_id_type=MESH,
        )

    def copies(sem, *pairs):
        return [pltpu.make_async_copy(src, dst, load_sems.at[sem]) for src, dst in pairs]

    new_loads = copies(0, (q_hbm, new_ref.at[0]), (nk_hbm, new_ref.at[1]), (nv_hbm, new_ref.at[2]))
    small = (
        copies(1, (lengths_hbm, lengths_ref)) + copies(2, (ids_hbm, ids_ref))
        + copies(3, (rw_hbm, rw_ref)) + copies(4, (hid_hbm, hid_ref))
    )
    gain_loads = copies(5, (gain_hbm, gains.at[0]), (score_hbm, gains.at[1]))
    proj_load = copies(6, (proj_hbm, proj_buf))
    expert_loads = copies(
        7, (eg_hbm.at[0], expert.at[0]), (eu_hbm.at[0], expert.at[1]), (ed_hbm.at[0], expert.at[2])
    )
    shared_loads = copies(
        8, (sg_hbm, shared_w.at[0]), (su_hbm, shared_w.at[1]), (sd_hbm, shared_w.at[2])
    )
    PAIR = 2

    def cache_load(hbm, buf, sem, b):
        rows_at = pl.ds(b, PAIR)
        return pltpu.make_async_copy(hbm.at[rows_at], buf.at[rows_at], sem.at[b // PAIR])

    k_load = [cache_load(k_hbm, k_buf, k_sem, b) for b in range(0, rows, PAIR)]
    v_load = [cache_load(v_hbm, v_buf, v_sem, b) for b in range(0, rows, PAIR)]
    queue = []
    for p in range(parts):
        pairs = range(p * toks // PAIR, (p + 1) * toks // PAIR)
        queue += [k_load[i] for i in pairs] + [v_load[i] for i in pairs]
        if p == 0:
            queue += proj_load
    queue += expert_loads + shared_loads
    issued = [0]

    def issue(upto):
        while issued[0] < min(upto, len(queue)):
            queue[issued[0]].start()
            issued[0] += 1

    def landed(copy):
        copy.wait()
        issue(next(i for i, c in enumerate(queue) if c is copy) + 1 + AHEAD)

    for load in new_loads + small + gain_loads:
        load.start()
    issue(AHEAD)
    barrier = pltpu.get_barrier_semaphore()
    for j, y in steps:
        pl.semaphore_signal(
            barrier, inc=1, device_id=(peer_rows[j], back_at[y]), device_id_type=MESH
        )
    pl.semaphore_signal(barrier, inc=1, device_id=(me_r, pair), device_id_type=MESH)

    pltpu.make_async_copy(new_ref, new_ref, load_sems.at[0]).wait()
    for load in small:
        load.wait()
    pltpu.make_async_copy(gains, gains, load_sems.at[5]).wait()

    span, width = k_buf.shape[1:]
    scale = HD ** (-0.5)
    group = max(8, width // HD)
    own_head = (
        lax.broadcasted_iota(jnp.int32, (group, width), 0)
        == lax.broadcasted_iota(jnp.int32, (group, width), 1) // HD
    )
    position = lax.broadcasted_iota(jnp.int32, (group, span), 1)
    queries = new_ref[0].astype(F32)
    own_keys = new_ref[1].astype(F32)
    own_values = new_ref[2].astype(F32)

    def score(b):
        spread = jnp.where(own_head, queries[b:b + 1, :], 0.0)
        scores = lax.dot_general(
            spread.astype(BF16), k_buf[b], ROWS_BY_ROWS, preferred_element_type=F32
        )
        own_score = jnp.sum(spread * own_keys[b:b + 1, :], axis=1, keepdims=True)
        scores = jnp.where(position < lengths_ref[b], scores, -1e30)
        highest = jnp.maximum(jnp.max(scores, axis=1, keepdims=True), own_score)
        exps = jnp.exp((scores - highest) * scale)
        own_exp = jnp.exp((own_score - highest) * scale)
        share = 1.0 / (jnp.sum(exps, axis=1, keepdims=True) + own_exp)
        own_part = jnp.sum(
            jnp.where(own_head, own_exp * own_values[b:b + 1, :], 0.0) * share,
            axis=0, keepdims=True,
        )
        return exps.astype(BF16), share, own_part

    def mix(b, scored):
        exps, share, own_part = scored
        mixed = jnp.dot(exps, v_buf[b], preferred_element_type=F32)
        mixed = jnp.where(own_head, mixed * share, 0.0)
        attended[b:b + 1, :] = jnp.sum(mixed, axis=0, keepdims=True) + own_part

    scored = {}

    def attend(score_pair, mix_pair):
        if score_pair is not None:
            landed(k_load[score_pair])
        if mix_pair is not None:
            landed(v_load[mix_pair])
        for i in range(PAIR):
            if score_pair is not None:
                b = score_pair * PAIR + i
                scored[b] = score(b)
            if mix_pair is not None:
                b = mix_pair * PAIR + i
                mix(b, scored.pop(b))

    def route_table():
        lane = lax.broadcasted_iota(jnp.int32, (rows, 128), 1).astype(F32)
        table = jnp.zeros((rows, 128), F32)
        route = rw_ref[...].astype(F32)
        ids = ids_ref[...].astype(F32)
        diagonal = (
            lax.broadcasted_iota(jnp.int32, (rows, rows), 0)
            == lax.broadcasted_iota(jnp.int32, (rows, rows), 1)
        )
        for k in range(ids.shape[0]):
            chosen = jnp.sum(jnp.where(diagonal, ids[k:k + 1, :], 0.0), axis=1, keepdims=True)
            share = jnp.sum(jnp.where(diagonal, route[k:k + 1, :], 0.0), axis=1, keepdims=True)
            table = table + jnp.where(chosen == lane, share, 0.0)
        w_own[...] = table

    def route_copies():
        for j in reversed(range(1, req_count)):
            remote(w_own, w_in.at[j - 1], w_sems.at[0], w_sems.at[1], peer_rows[j], me_h).start()

    def all_sent(ref, sem):
        remote(ref, ref, sem, sem, me_r, pair).wait_send()

    def all_here(ref, sem):
        remote(ref, ref, sem, sem, me_r, pair).wait_recv()

    def rows_of(p):
        return slice(p * toks, (p + 1) * toks)

    def pair_copy(p, src, dst, sem):
        return remote(
            src.at[p], dst.at[p], send_sem, part_sems.at[p, sem // 2], me_r, pair
        )

    kept = {}

    def project(p):
        mixed = attended[rows_of(p), :].astype(BF16)
        pair1_out[p] = jnp.dot(mixed, proj_buf[:, other], preferred_element_type=F32)
        pair_copy(p, pair1_out, pair1_in, 0).start()
        hidden = jnp.where(me_y == 0, hid_ref[:, own].astype(F32), 0.0)
        kept[p] = (
            jnp.dot(mixed, proj_buf[:, own], preferred_element_type=F32) + hidden[rows_of(p)]
        )

    def spread_out(p):
        pair_copy(p, pair1_out, pair1_in, 0).wait_recv()
        mine1[p] = (kept.pop(p) + pair1_in[p]).astype(BF16)
        for j, y in reversed(steps):
            remote(
                mine1.at[p], land1.at[p, j * lines + y - 1], send_sem,
                part_sems.at[p, 1], peer_rows[j], lines_at[y],
            ).start()

    def collect(p):
        all_here(land1.at[p], part_sems.at[p, 1])
        for j in range(req_count):
            total = None
            for y in range(lines):
                block = land1[p, j * lines + y - 1] if j + y > 0 else mine1[p]
                block = block.astype(F32)
                total = block if total is None else total + block
            resid = total.astype(BF16)
            fwd_out[p, j] = resid
            x_own[p, j * toks:(j + 1) * toks, :] = resid.astype(F32)
        pair_copy(p, fwd_out, fwd_in, 4).start()

    def half_terms(x, cols):
        square = jnp.sum(x * x, axis=1, keepdims=True)
        gained = (x * gains[0, :, cols]).astype(BF16)
        logit = jnp.sum(gained.astype(F32) * gains[1, :, cols], axis=1, keepdims=True)
        return [square, logit] + [
            lax.dot_general(gained, w[i, :, cols], ROWS_BY_ROWS, preferred_element_type=F32)
            for w in (expert, shared_w) for i in range(2)
        ]

    def experts(p):
        first = half_terms(x_own[p], own)
        if p > 0:
            give_back(p - 1)
        pair_copy(p, fwd_out, fwd_in, 4).wait_recv()
        for j in range(req_count):
            x_other[p, j * toks:(j + 1) * toks, :] = fwd_in[p, j].astype(F32)
        second = half_terms(x_other[p], other)
        square, logit, g, u, shared_g, shared_u = [a + b for a, b in zip(first, second)]
        inverse = lax.rsqrt(square / model + EPSILON)
        gate_scale = 1.0 / (1.0 + jnp.exp(-logit * inverse))
        lane = lax.broadcasted_iota(jnp.int32, w_part.shape[1:], 1)
        weight = jnp.sum(jnp.where(lane == me_r, w_part[p], 0.0), axis=1, keepdims=True)
        inner = (silu(g * inverse) * (u * (inverse * weight))).astype(BF16)
        hidden = (silu(shared_g * inverse) * (shared_u * (inverse * gate_scale))).astype(BF16)

        def down(cols):
            return (
                jnp.dot(inner, expert[2, :, cols], preferred_element_type=F32)
                + jnp.dot(hidden, shared_w[2, :, cols], preferred_element_type=F32)
            )

        pair2_out[p] = down(other).astype(BF16)
        pair_copy(p, pair2_out, pair2_in, 6).start()
        d_own[p] = down(own)

    def give_back(p):
        pair_copy(p, pair2_out, pair2_in, 6).wait_recv()
        d_own[p] = d_own[p] + pair2_in[p].astype(F32)
        for j in range(req_count):
            send2[p, j] = d_own[p, j * toks:(j + 1) * toks, :].astype(BF16)
        for r, h, j, slot in targets:
            remote(
                send2.at[p, j], land2.at[p, slot], send_sem, part_sems.at[p, 4], r, h
            ).start()

    def combine(p):
        total = fwd_out[p, 0].astype(F32) + d_own[p, 0:toks, :]
        all_here(land2.at[p], part_sems.at[p, 4])
        for i in range(land2.shape[1]):
            total = total + land2[p, i].astype(F32)
        fin_out[p] = total.astype(BF16)
        pair_copy(p, fin_out, fin_in, 10).start()

    def finish():
        for p in range(parts):
            pair_copy(p, fin_out, fin_in, 10).wait_recv()
        for cols, ref in ((own, fin_out), (other, fin_in)):
            blocks = [ref[p].astype(F32) for p in range(parts)]
            whole = blocks[0] if parts == 1 else jnp.concatenate(blocks, axis=0)
            out_ref[:, cols] = whole.astype(BF16)

    route_table()
    for p in range(parts):
        first, last = p * toks // PAIR, (p + 1) * toks // PAIR - 1
        attend(first, None)
        if p > 0:
            spread_out(p - 1)
        for i in range(first, last):
            attend(i + 1, i)
        attend(None, last)
        if p == 0:
            landed(proj_load[0])
            pl.semaphore_wait(barrier, len(steps) + 1)
        project(p)
        if p == 0:
            route_copies()
    spread_out(parts - 1)
    issue(len(queue))
    all_here(w_in, w_sems.at[1])
    for p in range(parts):
        for j in range(req_count):
            table = w_own if j == 0 else w_in.at[j - 1]
            w_part[p, j * toks:(j + 1) * toks, :] = table[rows_of(p), :]
    for p in range(parts):
        collect(p)
        if p == 0:
            pltpu.make_async_copy(expert, expert, load_sems.at[7]).wait()
            pltpu.make_async_copy(shared_w, shared_w, load_sems.at[8]).wait()
        experts(p)
    give_back(parts - 1)
    for p in range(parts):
        combine(p)
    finish()
    all_sent(w_in, w_sems.at[0])
    all_sent(tally, send_sem)


VMEM_SPEC = pl.BlockSpec(memory_space=pltpu.VMEM)
HBM_SPEC = pl.BlockSpec(memory_space=pltpu.HBM)


def per_device(
    req_count, head_count,
    hidden_in, queries, new_keys, new_values, key_cache, value_cache, lengths, out_proj,
    norm_gain, shared_gate, shared_up, shared_down, shared_score, expert_gate, expert_up,
    expert_down, expert_ids, route_weight,
):
    rows, model = hidden_in.shape
    span, width = key_cache.shape[1:]
    dma, vmem = pltpu.SemaphoreType.DMA, pltpu.VMEM
    parts, lines, half = PARTS, head_count // 2, model // 2
    toks = rows // parts
    tokens = req_count * toks
    return pl.pallas_call(
        functools.partial(layer_kernel, req_count, head_count),
        out_shape=pltpu.VMEM((rows, model), BF16),
        in_specs=[HBM_SPEC] * 18,
        out_specs=VMEM_SPEC,
        scratch_shapes=[
            pltpu.SMEM((rows,), jnp.int32),
            vmem((3, rows, width), BF16),
            vmem((rows, model), BF16),
            vmem((2, 1, model), F32),
            vmem(expert_ids.shape[::-1], jnp.int32),
            vmem(route_weight.shape[::-1], BF16),
            vmem((rows, span, width), BF16),
            vmem((rows, span, width), BF16),
            vmem(out_proj.shape, BF16),
            vmem((3,) + expert_down.shape[1:], BF16),
            vmem((3,) + shared_down.shape, BF16),
            dma((9,)), dma((rows // 2,)), dma((rows // 2,)),
            vmem((rows, width), F32),
            vmem((rows, 128), F32),
            vmem((req_count - 1, rows, 128), F32),
            vmem((parts, tokens, 128), F32),
            vmem((parts, tokens, half), F32),
            vmem((parts, tokens, half), F32),
            vmem((parts, tokens, half), F32),
            vmem((parts, toks, half), F32),
            vmem((parts, toks, half), F32),
            vmem((parts, toks, half), BF16),
            vmem((parts, req_count * lines - 1, toks, half), BF16),
            vmem((parts, req_count, toks, half), BF16),
            vmem((parts, req_count, toks, half), BF16),
            vmem((parts, tokens, half), BF16),
            vmem((parts, tokens, half), BF16),
            vmem((parts, req_count, toks, half), BF16),
            vmem((parts, req_count * lines - 1, toks, half), BF16),
            vmem((parts, toks, half), BF16),
            vmem((parts, toks, half), BF16),
            vmem((parts * (2 * (req_count * lines - 1) + 2 * req_count + 3), toks, half), BF16),
            dma((2,)), dma((parts, 6)), dma,
        ],
        compiler_params=pltpu.CompilerParams(
            vmem_limit_bytes=63 << 20, collective_id=0, has_side_effects=True
        ),
        name="layer",
    )(
        lengths, queries, new_keys, new_values, key_cache, value_cache, out_proj,
        hidden_in, norm_gain.reshape(1, model), shared_score.reshape(1, model),
        expert_ids.T, route_weight.T,
        shared_gate, shared_up, shared_down,
        jnp.swapaxes(expert_gate, 1, 2), jnp.swapaxes(expert_up, 1, 2), expert_down,
    )


def solution(mesh):
    in_specs = (
        P("req", None),
        P("req", "head"),
        P("req", "head"),
        P("req", "head"),
        P("req", None, "head"),
        P("req", None, "head"),
        P("req"),
        P("head", None),
        P(),
        P(("req", "head"), None),
        P(("req", "head"), None),
        P(("req", "head"), None),
        P(),
        P("req", None, "head"),
        P("req", None, "head"),
        P("req", "head", None),
        P("req", None),
        P("req", None),
    )
    body = functools.partial(per_device, mesh.shape["req"], mesh.shape["head"])
    return jax.shard_map(
        body, mesh=mesh, in_specs=in_specs, out_specs=P("req", None), check_vma=False
    )
```
